128 devices in a mesh: pool: 2 (over core), grp: 4 (over y), rep: 16 (over x, z).
Axes of the slice: x: 4, y: 4, z: 4, core: 2. Of those that a mesh axis runs over, the one named last changes fastest.
Arguments:
- queries: bfloat16 [512, 8192], P('pool', 'grp'), may hold values from -64 to 64
- keys: bfloat16 [16384, 512], P('rep', 'grp'), may hold values from -7 to 7
- values: bfloat16 [16384, 512], P('rep', 'grp'), may hold values from -6 to 6
- hidden_in: bfloat16 [512, 4096], P(('pool', 'grp', 'rep')), may hold values from -4 to 4
- o_weight: bfloat16 [8192, 4096], P('grp', 'rep'), may hold values from -0.125 to 0.125
- norm_gain: bfloat16 [4096], replicated, may hold values from 0.5 to 1.5
- routes: int32 [512, 8], P(('pool', 'grp', 'rep')), may hold values from 0 to 63, as said below
- route_weights: float32 [512, 8], P(('pool', 'grp', 'rep')), may hold values from 0.02 to 0.25
- w_gate: bfloat16 [64, 4096, 1536], P(('grp', 'rep'), None, 'pool'), may hold values from -0.09375 to 0.09375
- w_up: bfloat16 [64, 4096, 1536], P(('grp', 'rep'), None, 'pool'), may hold values from -0.09375 to 0.09375
- w_down: bfloat16 [64, 1536, 4096], P(('grp', 'rep'), 'pool'), may hold values from -0.15625 to 0.15625
Outputs:
- mid_rows: bfloat16 [512, 4096], P(('pool', 'grp', 'rep'))
- expert_mix: bfloat16 [512, 4096], P(('pool', 'grp', 'rep'))
The draws below stay inside these ranges and needn't reach their ends.
Inputs may be any that keep to these rules, and one draw needn't show every extreme that they name: `routes`: each row names 8 different experts. In the rows of one device each expert is named by no row or by exactly 2 rows, and one expert, the same on every device, is named by 2 rows on every device.
All inputs are finite; a program needn't handle non-finite values.
Results may differ from the reference program's by a relative error of at most 0.027.
Values may be sent and summed in bfloat16 or wider, within the bound.
A program may use at most 128 MiB of HBM per device.

```python
import math
import jax
import jax.numpy as jnp
from jax import lax

D = 4096
HEADS = 64
KV_HEADS = 4
HEAD_DIM = 128
EXPERT_FF = 1536
TOPK = 8
PREFIX = 16384
ROW_DEV = 4
EXPERTS = 64
ROWS = 512
CAP = 2
N_POOL = 2
N_GRP = 4
N_REP = 16


def unit_table(key):
    base_key = jax.random.fold_in(key, 11)
    unit_keys = jnp.clip(jax.random.normal(base_key, (PREFIX, KV_HEADS * HEAD_DIM), jnp.float32), -5.0, 5.0)
    return unit_keys


def key_ramp():
    places = jnp.arange(PREFIX, dtype=jnp.float32)
    return 0.8 + 0.6 * places / max(PREFIX - 1, 1)


def draw_keys(key, part):
    return (unit_table(key) * key_ramp()[:, None]).astype(jnp.bfloat16)


def draw_queries(key, part):
    query_shape = (ROWS, HEADS * HEAD_DIM)
    base_key = jax.random.fold_in(key, 23)
    result = jnp.clip(2.0 * jax.random.normal(base_key, query_shape, jnp.float32), -10.0, 10.0)
    return result.astype(jnp.bfloat16)


def draw_routes(key, part):
    block_count = ROWS // ROW_DEV
    hot_key, rest_key = jax.random.split(jax.random.fold_in(key, 5))
    hot_expert = jax.random.randint(hot_key, (), 0, EXPERTS)
    block_keys = jax.random.split(rest_key, block_count)
    slot_index = (jnp.arange(TOPK, dtype=jnp.int32)[None, :] * ROW_DEV + jnp.arange(ROW_DEV, dtype=jnp.int32)[:, None]) // CAP

    def one_block(block_key):
        shuffle_key, row_key, column_key = jax.random.split(block_key, 3)
        shuffle = jax.random.randint(shuffle_key, (EXPERTS,), 0, 1 << 20) * EXPERTS + jnp.arange(EXPERTS, dtype=jnp.int32)
        shuffle = jnp.where(jnp.arange(EXPERTS, dtype=jnp.int32) == hot_expert, -1, shuffle)
        expert_order = jnp.argsort(shuffle).astype(jnp.int32)
        chosen = expert_order[slot_index]
        row_order = jax.random.permutation(row_key, ROW_DEV)
        chosen = chosen[row_order]
        column_score = jax.random.randint(column_key, (ROW_DEV, TOPK), 0, 1 << 20) * TOPK + jnp.arange(TOPK, dtype=jnp.int32)[None, :]
        column_order = jnp.argsort(column_score, axis=1)
        return jnp.take_along_axis(chosen, column_order, axis=1).astype(jnp.int32)
    return jax.vmap(one_block)(block_keys).reshape(ROWS, TOPK)


def level_of(stream_key, dims, cuts, low, top_value):
    def one(dim, blocks):
        steps = jax.random.uniform(jax.random.fold_in(jax.random.fold_in(stream_key, 6), dim), (blocks,), jnp.float32, low / len(cuts), top_value / len(cuts))
        return jnp.repeat(jnp.exp(steps), dims[dim] // blocks).reshape((-1,) + (1,) * (len(dims) - dim - 1))

    gain = one(*cuts[0])
    for cut in cuts[1:]:
        gain = gain * one(*cut)
    return gain


def bell_draw(key, shape, spread, reach, cuts=(), kind=jnp.bfloat16):
    level = level_of(key, shape, cuts, -0.22, 0.18) if cuts else 1.0
    values = jax.random.normal(key, shape, jnp.float32) * spread * level
    return jnp.minimum(jnp.maximum(values, -reach), reach).astype(kind)


def setup_inputs(seed: int = 0) -> dict:
    splits = jax.random.split(jax.random.key(seed), 12)
    queries = draw_queries(jax.random.fold_in(splits[11], 71), 0)
    keys = draw_keys(jax.random.fold_in(splits[11], 71), 0)
    values = bell_draw(splits[2], (PREFIX, KV_HEADS * HEAD_DIM), 1.0, 6.0, ((0, 16), (1, 4)))
    hidden_in = bell_draw(splits[3], (ROWS, D), 0.5, 4.0, ((0, 128),))
    o_weight = bell_draw(splits[4], (HEADS * HEAD_DIM, D), (HEADS * HEAD_DIM // 4) ** -0.5, 0.125, ((0, 4), (1, 16)))
    norm_gain = jnp.clip(1.0 + 0.1 * jax.random.normal(splits[5], (D,), jnp.float32), 0.5, 1.5).astype(jnp.bfloat16)
    routes = draw_routes(jax.random.fold_in(splits[11], 71), 0)
    route_weights = jnp.clip(jnp.exp(math.log(0.25) - 2.5257287 * jax.random.uniform(splits[7], (ROWS, TOPK), jnp.float32) ** level_of(splits[7], (ROWS, TOPK), ((0, 128),), -0.2, 0.2)), 0.02, 0.25)
    w_gate = bell_draw(splits[8], (EXPERTS, D, EXPERT_FF), D ** -0.5, 0.09375, ((0, 64), (2, 2)))
    w_up = bell_draw(splits[9], (EXPERTS, D, EXPERT_FF), D ** -0.5, 0.09375, ((0, 64), (2, 2)))
    w_down = bell_draw(splits[10], (EXPERTS, EXPERT_FF, D), EXPERT_FF ** -0.5, 0.15625, ((0, 64), (1, 2)))
    return dict(queries=queries, keys=keys, values=values, hidden_in=hidden_in, o_weight=o_weight, norm_gain=norm_gain, routes=routes, route_weights=route_weights, w_gate=w_gate, w_up=w_up, w_down=w_down)


def expert_apply(rows_in, gate_w, up_w, down_w):
    gate_proj = jnp.dot(rows_in, gate_w, preferred_element_type=jnp.float32)
    upper = jnp.dot(rows_in, up_w, preferred_element_type=jnp.float32)
    activated = (jax.nn.silu(gate_proj) * upper).astype(jnp.bfloat16)
    return jnp.dot(activated, down_w, preferred_element_type=jnp.float32)

def reference(queries, keys, values, hidden_in, o_weight, norm_gain, routes, route_weights, w_gate, w_up, w_down):
    group_size = HEADS // KV_HEADS
    total_rows = queries.shape[0]
    block_rows = 32
    score_scale = HEAD_DIM ** (-0.5)
    key_heads = keys.astype(jnp.float32).reshape(PREFIX, KV_HEADS, HEAD_DIM)
    value_heads = values.astype(jnp.float32).reshape(PREFIX, KV_HEADS, HEAD_DIM)
    query_blocks = queries.reshape(total_rows // block_rows, block_rows, KV_HEADS, group_size, HEAD_DIM)

    def attend(query_block):
        scores = jnp.einsum('rkgd,pkd->rkgp', query_block.astype(jnp.float32), key_heads) * score_scale
        top_score = lax.optimization_barrier(jnp.max(scores, axis=-1, keepdims=True))
        exp_scores = jnp.exp(scores - top_score)
        exp_total = lax.optimization_barrier(jnp.sum(exp_scores, axis=-1))
        probs = lax.optimization_barrier(exp_scores.astype(jnp.bfloat16)).astype(jnp.float32)
        weighted = jnp.einsum('rkgp,pkd->rkgd', probs, value_heads)
        return (weighted / exp_total[..., None]).astype(jnp.bfloat16)
    attention = lax.map(attend, query_blocks).reshape(total_rows, HEADS * HEAD_DIM)
    attn_proj = jnp.dot(attention, o_weight, preferred_element_type=jnp.float32).astype(jnp.bfloat16)
    attn_proj = lax.optimization_barrier(attn_proj)
    mid_rows = (hidden_in.astype(jnp.float32) + attn_proj.astype(jnp.float32)).astype(jnp.bfloat16)
    mid_wide = lax.optimization_barrier(mid_rows).astype(jnp.float32)
    inverse = lax.rsqrt(lax.optimization_barrier(jnp.mean(mid_wide * mid_wide, axis=-1, keepdims=True)) + 1e-06)
    normed = (mid_wide * inverse * norm_gain.astype(jnp.float32)).astype(jnp.bfloat16)
    device_count = N_POOL * N_GRP * N_REP
    assigned = ROW_DEV * TOPK
    expert_ids = routes.reshape(device_count, assigned)
    member = (expert_ids[..., None] == jnp.arange(EXPERTS, dtype=jnp.int32)[None, None, :]).astype(jnp.int32)
    position = lax.optimization_barrier(jnp.sum(jnp.cumsum(member, axis=1) * member, axis=-1)) - 1
    slot_rank = (jnp.arange(device_count, dtype=jnp.int32)[:, None] * CAP + position).astype(jnp.int32)
    row_ids = (jnp.arange(device_count, dtype=jnp.int32)[:, None] * ROW_DEV + jnp.arange(assigned, dtype=jnp.int32)[None, :] // TOPK).astype(jnp.int32)
    slot_width = device_count * CAP
    table_rows = jnp.zeros((EXPERTS, slot_width), jnp.int32).at[expert_ids, slot_rank].set(row_ids)
    used_rows = jnp.zeros((EXPERTS, slot_width), jnp.float32).at[expert_ids, slot_rank].set(1.0)

    def one_expert(operands):
        table_one, used_one, gate_w, up_w, down_w = operands
        rows_in = (normed[table_one].astype(jnp.float32) * used_one[:, None]).astype(jnp.bfloat16)
        return expert_apply(rows_in, gate_w, up_w, down_w).astype(jnp.bfloat16)
    expert_out = lax.map(one_expert, (table_rows, used_rows, w_gate, w_up, w_down))
    expert_out = lax.optimization_barrier(expert_out)
    picked = expert_out[expert_ids, slot_rank].reshape(total_rows, TOPK, D)
    expert_mix = lax.optimization_barrier(jnp.sum(route_weights[..., None] * picked.astype(jnp.float32), axis=1)).astype(jnp.bfloat16)
    return (mid_rows, expert_mix)
```

```python
import jax
import jax.numpy as jnp
from jax import lax
from jax.sharding import PartitionSpec as P

HEAD_DIM = 128


def expert_apply(rows_in, gate_w, up_w, down_w):
    gate_proj = jnp.dot(rows_in, gate_w, preferred_element_type=jnp.float32)
    upper = jnp.dot(rows_in, up_w, preferred_element_type=jnp.float32)
    activated = (jax.nn.silu(gate_proj) * upper).astype(jnp.bfloat16)
    return jnp.dot(activated, down_w, preferred_element_type=jnp.float32)


def per_device(
    queries,
    keys,
    values,
    hidden_in,
    o_weight,
    norm_gain,
    routes,
    route_weights,
    w_gate,
    w_up,
    w_down,
):
    kv_local = keys.shape[1] // HEAD_DIM
    heads_local = queries.shape[1] // HEAD_DIM
    group_size = heads_local // kv_local
    batch_rows = queries.shape[0]
    key_span = keys.shape[0]
    per_block = min(4, group_size)
    blocks = group_size // per_block
    score_scale = HEAD_DIM ** (-0.5)
    query_blocks = jnp.moveaxis(
        queries.reshape(batch_rows, kv_local, blocks, per_block, HEAD_DIM), 2, 0
    )
    key_heads = keys.reshape(key_span, kv_local, HEAD_DIM)
    value_heads = values.reshape(key_span, kv_local, HEAD_DIM)

    def local_part(query_block):
        scores = (
            jnp.einsum("rkhd,pkd->rkhp", query_block, key_heads, preferred_element_type=jnp.float32)
            * score_scale
        )
        top_score = jnp.max(scores, axis=-1)
        exp_scores = jnp.exp(scores - top_score[..., None])
        exp_total = jnp.sum(exp_scores, axis=-1)
        weighted = jnp.einsum(
            "rkhp,pkd->rkhd",
            exp_scores.astype(jnp.bfloat16),
            value_heads,
            preferred_element_type=jnp.float32,
        )
        return (top_score, exp_total, weighted)

    top_part, total_part, value_part = lax.map(local_part, query_blocks)
    rep_size = lax.axis_size("rep")
    share = batch_rows // rep_size
    rows_heads = share * heads_local

    def by_peer(part):
        part = jnp.moveaxis(part, 0, 2)
        return part.reshape((rep_size, rows_heads) + part.shape[4:])

    stats = jnp.stack([by_peer(top_part), by_peer(total_part)], axis=1)
    payload = jnp.concatenate(
        [by_peer(value_part), stats.reshape(rep_size, -1, HEAD_DIM)], axis=1
    )
    payload = lax.all_to_all(payload, "rep", split_axis=0, concat_axis=0, tiled=True)
    weighted = payload[:, :rows_heads]
    stats = payload[:, rows_heads:].reshape(rep_size, 2, rows_heads)
    joint_top = jnp.max(stats[:, 0], axis=0)
    factors = jnp.exp(stats[:, 0] - joint_top)
    exp_total = jnp.sum(stats[:, 1] * factors, axis=0)
    weighted = jnp.sum(weighted * factors[..., None], axis=0)
    attention = (weighted / exp_total[:, None]).astype(jnp.bfloat16)
    attention = lax.all_gather(
        attention.reshape(share, heads_local * HEAD_DIM), "rep", axis=0, tiled=True
    )
    head_total = lax.psum_scatter(
        jnp.dot(attention, o_weight, preferred_element_type=jnp.float32),
        "grp",
        scatter_dimension=0,
        tiled=True,
    )
    attn_proj = head_total.astype(jnp.bfloat16)
    full_rows = lax.all_to_all(attn_proj, "rep", split_axis=0, concat_axis=1, tiled=True)
    mid_rows = (hidden_in.astype(jnp.float32) + full_rows.astype(jnp.float32)).astype(jnp.bfloat16)
    mid_wide = lax.optimization_barrier(mid_rows).astype(jnp.float32)
    inverse = lax.rsqrt(jnp.mean(mid_wide * mid_wide, axis=-1, keepdims=True) + 1e-06)
    normed = (mid_wide * inverse * norm_gain.astype(jnp.float32)).astype(jnp.bfloat16)
    row_dev, topk = routes.shape
    model_width = hidden_in.shape[1]
    group_count = lax.axis_size("grp")
    rep_count = lax.axis_size("rep")
    experts = group_count * rep_count
    capacity = max(2, 2 * row_dev * topk // experts)
    flat_routes = routes.reshape(-1)
    order = jnp.arange(flat_routes.shape[0], dtype=jnp.int32)
    same_before = (flat_routes[:, None] == flat_routes[None, :]) & (order[None, :] < order[:, None])
    position = jnp.sum(same_before.astype(jnp.int32), axis=1)
    slot_index = flat_routes * capacity + position
    chooser = jnp.any(
        jnp.arange(experts * capacity, dtype=jnp.int32)[:, None, None]
        == slot_index.reshape(row_dev, topk)[None, :, :],
        axis=2,
    ).astype(jnp.bfloat16)
    outgoing = jnp.dot(chooser, normed, preferred_element_type=jnp.float32).astype(jnp.bfloat16)
    arrived = lax.all_to_all(
        outgoing.reshape(experts, capacity, model_width),
        ("grp", "rep"),
        split_axis=0,
        concat_axis=0,
        tiled=True,
    )
    sources = arrived.shape[0]
    slots_here = arrived.shape[1]
    combined = expert_apply(
        lax.all_gather(arrived.reshape(-1, model_width), "pool", axis=0, tiled=True),
        w_gate[0],
        w_up[0],
        w_down[0],
    )
    served = (
        lax.psum_scatter(combined, "pool", scatter_dimension=0, tiled=True)
        .astype(jnp.bfloat16)
        .reshape(sources, slots_here, model_width)
    )
    returned = lax.all_to_all(served, ("grp", "rep"), split_axis=0, concat_axis=0, tiled=True)
    returned = returned.reshape(-1, model_width)
    picked = jnp.take(returned, slot_index, axis=0).reshape(row_dev, topk, model_width)
    expert_mix = jnp.sum(route_weights[..., None] * picked.astype(jnp.float32), axis=1).astype(
        jnp.bfloat16
    )
    return (mid_rows, expert_mix)


def solution(mesh):
    return jax.shard_map(
        per_device,
        mesh=mesh,
        in_specs=(
            P("pool", "grp"),
            P("rep", "grp"),
            P("rep", "grp"),
            P(("pool", "grp", "rep"), None),
            P("grp", "rep"),
            P(),
            P(("pool", "grp", "rep"), None),
            P(("pool", "grp", "rep"), None),
            P(("grp", "rep"), None, "pool"),
            P(("grp", "rep"), None, "pool"),
            P(("grp", "rep"), "pool", None),
        ),
        out_specs=(P(("pool", "grp", "rep"), None), P(("pool", "grp", "rep"), None)),
        check_vma=False,
    )
```

```python
import functools

import jax
import jax.numpy as jnp
from jax import lax
from jax.experimental import pallas as pl
from jax.experimental.pallas import tpu as pltpu
from jax.sharding import PartitionSpec as P

HEAD_DIM = 128
CHUNKS = 8
SLOTS = 2
PAIR = CHUNKS * SLOTS
LOG2E = 1.4426950408889634
MESH = pl.DeviceIdType.MESH
BF = jnp.bfloat16
F32 = jnp.float32


def remote(src, dst, send, recv, where):
    return pltpu.make_async_remote_copy(
        src_ref=src,
        dst_ref=dst,
        send_sem=send,
        recv_sem=recv,
        device_id=where,
        device_id_type=MESH,
    )


def layer(
    G, R,
    q_hbm, k_hbm, v_hbm, ow_hbm, hidden_ref, gain_ref, sel_ref, comb_ref, wg_hbm, wu_hbm, wd_hbm,
    mid_ref, mix_ref,
    q_s, k_s, v_s, vt_s, ow_s, wg_s, wu_s, wd_s, load_sem,
    part_s, stat_s, part_r, stat_r, attn_s,
    proj_f, proj_s, proj_r, cols_s, cols_r,
    disp_s, disp_r, rows_s, act_s, half_s, half_r, sum_s, back_s, back_r,
    part_ss, part_rs, stat_ss, stat_rs, attn_ss, attn_rs,
    proj_ss, proj_rs, cols_ss, cols_rs, disp_ss, disp_rs,
    rows_ss, rows_rs, half_ss, half_rs, back_ss, back_rs,
):
    pool, grp, rep = lax.axis_index("pool"), lax.axis_index("grp"), lax.axis_index("rep")
    E = G * R
    me = grp * R + rep
    sibling = (1 - pool, grp, rep)

    loads = [
        pltpu.make_async_copy(src, dst, load_sem.at[i])
        for i, (src, dst) in enumerate(
            (
                (q_hbm, q_s),
                (k_hbm, k_s),
                (v_hbm, v_s),
                (ow_hbm, ow_s),
                (wg_hbm, wg_s),
                (wu_hbm, wu_s),
                (wd_hbm, wd_s),
            )
        )
    ]
    for load in loads:
        load.start()

    barrier = pltpu.get_barrier_semaphore()

    def greet(d, carry):
        there = lax.rem(me + d, E)
        pl.semaphore_signal(
            barrier, inc=1, device_id=(pool, there // R, lax.rem(there, R)), device_id_type=MESH
        )
        return carry

    lax.fori_loop(1, E, greet, 0)
    pl.semaphore_signal(barrier, inc=1, device_id=sibling, device_id_type=MESH)

    for load in loads[:3]:
        load.wait()
    vt_s[...] = v_s[...].astype(F32).T.astype(BF)
    pl.semaphore_wait(barrier, E)

    rows_all, width = q_s.shape
    heads = width // HEAD_DIM
    share = rows_all // R
    lanes = share * heads
    scale = LOG2E * HEAD_DIM ** (-0.5)

    def part_copy(s):
        where = (pool, grp, lax.rem(rep + 1 + s, R))
        return (
            remote(part_s.at[s], part_r.at[s], part_ss.at[s], part_rs.at[s], where),
            remote(stat_s.at[s], stat_r.at[s], stat_ss.at[s], stat_rs.at[s], where),
        )

    def attend(s, carry):
        peer = lax.rem(rep + 1 + s, R)
        block = pl.ds(pl.multiple_of(peer * share, share), share)
        query = jnp.concatenate(
            [q_s[block, h * HEAD_DIM : (h + 1) * HEAD_DIM] for h in range(heads)], axis=0
        )
        scores = lax.dot_general(
            k_s[...], query, (((1,), (1,)), ((), ())), preferred_element_type=F32
        )
        top = jnp.max(scores, axis=0, keepdims=True)
        probs = jnp.exp2((scores - top) * scale)
        total = jnp.sum(probs, axis=0, keepdims=True)
        part = jnp.dot(vt_s[...], probs.astype(BF), preferred_element_type=F32)
        part_s[s] = part.astype(BF)
        first = lax.broadcasted_iota(jnp.int32, (8, lanes), 0) < 4
        stat_s[s] = jnp.where(first, top, total)

        @pl.when(s < R - 1)
        def _():
            for copy in part_copy(s):
                copy.start()

        return carry

    lax.fori_loop(0, R, attend, 0)

    def part_wait(s, carry):
        for copy in part_copy(s):
            copy.wait()
        return carry

    lax.fori_loop(0, R - 1, part_wait, 0)

    stats = [stat_r[s] for s in range(R - 1)] + [stat_s[R - 1]]
    top = functools.reduce(jnp.maximum, [stat[0:1] for stat in stats])
    factors = [jnp.exp2((stat[0:1] - top) * scale) for stat in stats]
    total = functools.reduce(
        jnp.add, [stat[4:5] * factor for stat, factor in zip(stats, factors)]
    )
    weighted = part_s[R - 1].astype(F32) * factors[R - 1]
    for s in range(R - 1):
        weighted += part_r[s].astype(F32) * factors[s]
    attention = (weighted / total).T.astype(BF)
    mine = pl.ds(pl.multiple_of(rep * share, share), share)
    for h in range(heads):
        attn_s[mine, h * HEAD_DIM : (h + 1) * HEAD_DIM] = attention[h * share : (h + 1) * share]

    def attn_copy(d, block):
        at = attn_s.at[pl.ds(pl.multiple_of(block * share, share), share)]
        where = (pool, grp, lax.rem(rep + d, R))
        return remote(at, at, attn_ss.at[d - 1], attn_rs.at[d - 1], where)

    def attn_start(d, carry):
        attn_copy(d, rep).start()
        return carry

    def attn_recv(d, carry):
        attn_copy(d, lax.rem(rep - d + R, R)).wait_recv()
        return carry

    lax.fori_loop(1, R, attn_start, 0)
    lax.fori_loop(1, R, attn_recv, 0)
    loads[3].wait()
    proj_f[...] = jnp.dot(attn_s[...], ow_s[...], preferred_element_type=F32)

    tall = rows_all // G
    for g in range(G):
        proj_s[g] = proj_f[g * tall : (g + 1) * tall].astype(BF)

    def proj_copy(d):
        there = lax.rem(grp + d, G)
        return remote(
            proj_s.at[there], proj_r.at[d - 1], proj_ss.at[d - 1], proj_rs.at[d - 1],
            (pool, there, rep),
        )

    for d in range(1, G):
        proj_copy(d).start()
    summed = proj_f[pl.ds(pl.multiple_of(grp * tall, tall), tall), :]
    for d in range(1, G):
        proj_copy(d).wait_recv()
        summed = summed + proj_r[d - 1].astype(F32)
    summed = summed.astype(BF).astype(F32)
    few = tall // R
    for j in range(R):
        cols_s[j] = summed[j * few : (j + 1) * few]

    def cols_copy(d, src, dst):
        where = (pool, grp, lax.rem(rep + d, R))
        return remote(
            cols_s.at[src], cols_r.at[dst], cols_ss.at[d - 1], cols_rs.at[d - 1], where
        )

    def cols_start(d, carry):
        cols_copy(d, lax.rem(rep + d, R), rep).start()
        return carry

    def cols_recv(d, carry):
        cols_copy(d, rep, lax.rem(rep - d + R, R)).wait_recv()
        return carry

    lax.fori_loop(1, R, cols_start, 0)
    cols_r[rep] = cols_s[rep]
    lax.fori_loop(1, R, cols_recv, 0)

    projected = jnp.concatenate([cols_r[j] for j in range(R)], axis=1)
    mid = (hidden_ref[...].astype(F32) + projected).astype(BF)
    mid_ref[...] = mid
    wide = mid.astype(F32)
    inverse = lax.rsqrt(jnp.mean(wide * wide, axis=-1, keepdims=True) + 1e-06)
    normed = wide * inverse * gain_ref[...].astype(F32)
    piece = normed.shape[1] // CHUNKS
    pieces = jnp.concatenate(
        [normed[:, c * piece : (c + 1) * piece] for c in range(CHUNKS)], axis=0
    ).astype(BF)

    tile = R * PAIR

    def fill(t, carry):
        chosen = jnp.dot(
            sel_ref[pl.ds(pl.multiple_of(t * tile, tile), tile), :],
            pieces,
            preferred_element_type=F32,
        )
        disp_s[pl.ds(t * R, R)] = chosen.astype(BF).reshape(R, PAIR, piece)
        return carry

    lax.fori_loop(0, G, fill, 0)

    def pair_copy(src, dst, send, recv, d, a, b):
        there = lax.rem(me + d, E)
        where = (pool, there // R, lax.rem(there, R))
        return remote(src.at[a], dst.at[b], send.at[d - 1], recv.at[d - 1], where)

    def disp_copy(d, a, b):
        return pair_copy(disp_s, disp_r, disp_ss, disp_rs, d, a, b)

    def back_copy(d, a, b):
        return pair_copy(back_s, back_r, back_ss, back_rs, d, a, b)

    def disp_start(d, carry):
        disp_copy(d, lax.rem(me + d, E), me).start()
        return carry

    lax.fori_loop(1, E, disp_start, 0)
    disp_r[me] = disp_s[me]

    row = lax.broadcasted_iota(jnp.int32, (tile, tile), 0)
    col = lax.broadcasted_iota(jnp.int32, (tile, tile), 1)
    pairs = R * SLOTS

    def moved(i):
        return lax.rem(i, pairs) // SLOTS * PAIR + i // pairs * SLOTS + lax.rem(i, SLOTS)

    gather = jnp.where(col == moved(row), 1.0, 0.0).astype(BF)
    spread = jnp.where(row == moved(col), 1.0, 0.0).astype(BF)

    def rows_copy(i, t):
        at = rows_s.at[pl.ds(pl.multiple_of(pool * (E * SLOTS) + t * pairs, pairs), pairs)]
        return remote(at, at, rows_ss.at[i], rows_rs.at[i], sibling)

    def collect(i, carry):
        t = lax.rem(grp + i, G)

        def arrive(j, inner):
            source = t * R + j
            d = lax.rem(me - source + E, E)

            @pl.when(d != 0)
            def _():
                disp_copy(d, me, source).wait_recv()

            return inner

        lax.fori_loop(0, R, arrive, 0)
        arrived = disp_r[pl.ds(t * R, R)].reshape(tile, piece)
        ordered = jnp.dot(gather, arrived, preferred_element_type=F32).astype(BF)
        at = pl.ds(pl.multiple_of(pool * (E * SLOTS) + t * pairs, pairs), pairs)
        for c in range(CHUNKS):
            rows_s[at, c * piece : (c + 1) * piece] = ordered[c * pairs : (c + 1) * pairs]
        rows_copy(i, t).start()
        return carry

    lax.fori_loop(0, G, collect, 0)

    def rows_recv(i, carry):
        t = lax.rem(grp + i, G)
        at = rows_s.at[pl.ds(pl.multiple_of((1 - pool) * (E * SLOTS) + t * pairs, pairs), pairs)]
        remote(at, at, rows_ss.at[i], rows_rs.at[i], sibling).wait_recv()
        return carry

    lax.fori_loop(0, G, rows_recv, 0)
    loads[4].wait()
    loads[5].wait()
    hidden = act_s.shape[1]
    step = min(256, hidden)

    def expand(n, carry):
        at = pl.ds(pl.multiple_of(n * step, step), step)
        gate = jnp.dot(rows_s[...], wg_s[0, :, at], preferred_element_type=F32)
        upper = jnp.dot(rows_s[...], wu_s[0, :, at], preferred_element_type=F32)
        act_s[:, at] = (gate / (1.0 + jnp.exp(-gate)) * upper).astype(BF)
        return carry

    lax.fori_loop(0, hidden // step, expand, 0)
    loads[6].wait()
    side = E * SLOTS

    def half_copy(n):
        return remote(
            half_s.at[n, 1 - pool], half_r.at[n], half_ss.at[n], half_rs.at[n], sibling
        )

    def contract(n, carry):
        at = pl.ds(pl.multiple_of(n * piece, piece), piece)
        out = jnp.dot(act_s[...], wd_s[0, :, at], preferred_element_type=F32)
        half_s[n, 0] = out[:side].astype(BF)
        half_s[n, 1] = out[side:].astype(BF)
        half_copy(n).start()
        return carry

    lax.fori_loop(0, CHUNKS, contract, 0)

    def merge(n, carry):
        half_copy(n).wait_recv()
        sum_s[n] = (half_s[n, pool].astype(F32) + half_r[n].astype(F32)).astype(BF)
        return carry

    lax.fori_loop(0, CHUNKS, merge, 0)

    def give_back(i, carry):
        t = lax.rem(grp + i, G)
        at = pl.ds(pl.multiple_of(t * pairs, pairs), pairs)
        stacked = sum_s[:, at, :].reshape(tile, piece)
        out = jnp.dot(spread, stacked, preferred_element_type=F32).astype(BF)
        back_s[pl.ds(t * R, R)] = out.reshape(R, PAIR, piece)

        def send(j, inner):
            there = t * R + j
            d = lax.rem(there - me + E, E)

            @pl.when(d != 0)
            def _():
                back_copy(d, there, me).start()

            return inner

        lax.fori_loop(0, R, send, 0)
        return carry

    lax.fori_loop(0, G, give_back, 0)
    back_r[me] = back_s[me]

    def back_recv(d, carry):
        back_copy(d, me, lax.rem(me - d + E, E)).wait_recv()
        return carry

    lax.fori_loop(1, E, back_recv, 0)
    weights = comb_ref[...]
    high = weights.astype(BF)
    low = (weights - high.astype(F32)).astype(BF)
    returned = back_r[...].reshape(E * PAIR, piece)
    mixed = jnp.dot(high, returned, preferred_element_type=F32) + jnp.dot(
        low, returned, preferred_element_type=F32
    )
    few = mix_ref.shape[0]
    for c in range(CHUNKS):
        mix_ref[:, c * piece : (c + 1) * piece] = mixed[c * few : (c + 1) * few].astype(BF)

    def rep_sent(d, carry):
        attn_copy(d, rep).wait_send()
        cols_copy(d, lax.rem(rep + d, R), rep).wait_send()
        return carry

    lax.fori_loop(1, R, rep_sent, 0)
    for d in range(1, G):
        proj_copy(d).wait_send()

    def pair_sent(d, carry):
        there = lax.rem(me + d, E)
        disp_copy(d, there, me).wait_send()
        back_copy(d, there, me).wait_send()
        return carry

    lax.fori_loop(1, E, pair_sent, 0)
    for i in range(G):
        rows_copy(i, lax.rem(grp + i, G)).wait_send()
    for n in range(CHUNKS):
        half_copy(n).wait_send()


def per_device(
    G, R,
    queries, keys, values, hidden_in, o_weight, norm_gain, routes, route_weights,
    w_gate, w_up, w_down,
):
    E = G * R
    rows_all, width = queries.shape
    span = keys.shape[0]
    few, model = hidden_in.shape
    block = o_weight.shape[1]
    hidden = w_gate.shape[2]
    heads = width // HEAD_DIM
    share = rows_all // R
    lanes = share * heads
    piece = model // CHUNKS
    tall = rows_all // G
    side = E * SLOTS

    hits = (routes[:, :, None] == jnp.arange(E, dtype=jnp.int32)).astype(F32)
    named = jnp.sum(hits, axis=1)
    weight = jnp.sum(hits * route_weights[:, :, None], axis=1)
    before = jnp.stack(
        [jnp.sum(named[:r], axis=0) if r else jnp.zeros_like(named[0]) for r in range(few)]
    )
    slot = jnp.arange(SLOTS, dtype=F32)[None, None, :]
    taken = jnp.where(before[:, :, None] == slot, named[:, :, None], 0.0)
    same = jnp.eye(CHUNKS, dtype=F32)
    sel = (
        jnp.transpose(taken, (1, 2, 0))[:, None, :, None, :] * same[None, :, None, :, None]
    ).reshape(E * PAIR, CHUNKS * few)
    comb = (
        (taken * weight[:, :, None])[None, :, :, None, :] * same[:, None, None, :, None]
    ).reshape(CHUNKS * few, E * PAIR)

    vmem = pl.BlockSpec(memory_space=pltpu.VMEM)
    anywhere = pl.BlockSpec(memory_space=pl.ANY)
    dma = pltpu.SemaphoreType.DMA
    scratch = [
        pltpu.VMEM(queries.shape, BF),
        pltpu.VMEM(keys.shape, BF),
        pltpu.VMEM(values.shape, BF),
        pltpu.VMEM((HEAD_DIM, span), BF),
        pltpu.VMEM(o_weight.shape, BF),
        pltpu.VMEM(w_gate.shape, BF),
        pltpu.VMEM(w_up.shape, BF),
        pltpu.VMEM(w_down.shape, BF),
        dma((7,)),
        pltpu.VMEM((R, HEAD_DIM, lanes), BF),
        pltpu.VMEM((R, 8, lanes), F32),
        pltpu.VMEM((R - 1, HEAD_DIM, lanes), BF),
        pltpu.VMEM((R - 1, 8, lanes), F32),
        pltpu.VMEM((rows_all, width), BF),
        pltpu.VMEM((rows_all, block), F32),
        pltpu.VMEM((G, tall, block), BF),
        pltpu.VMEM((G - 1, tall, block), BF),
        pltpu.VMEM((R, few, block), F32),
        pltpu.VMEM((R, few, block), F32),
        pltpu.VMEM((E, PAIR, piece), BF),
        pltpu.VMEM((E, PAIR, piece), BF),
        pltpu.VMEM((2 * side, model), BF),
        pltpu.VMEM((2 * side, hidden), BF),
        pltpu.VMEM((CHUNKS, 2, side, piece), BF),
        pltpu.VMEM((CHUNKS, side, piece), BF),
        pltpu.VMEM((CHUNKS, side, piece), BF),
        pltpu.VMEM((E, PAIR, piece), BF),
        pltpu.VMEM((E, PAIR, piece), BF),
    ]
    for count in (R - 1, R - 1, R - 1, G - 1, R - 1, E - 1, G, CHUNKS, E - 1):
        scratch += [dma((count,)), dma((count,))]
    return pl.pallas_call(
        functools.partial(layer, G, R),
        out_shape=[jax.ShapeDtypeStruct(hidden_in.shape, BF)] * 2,
        in_specs=[anywhere] * 4 + [vmem] * 4 + [anywhere] * 3,
        out_specs=[vmem] * 2,
        scratch_shapes=scratch,
        compiler_params=pltpu.CompilerParams(
            collective_id=0, has_side_effects=True, vmem_limit_bytes=58 << 20
        ),
        name="decode_layer",
    )(
        queries, keys, values, o_weight,
        hidden_in, norm_gain.reshape(1, model), sel.astype(BF), comb,
        w_gate, w_up, w_down,
    )


def solution(mesh):
    rows = P(("pool", "grp", "rep"), None)
    return jax.shard_map(
        functools.partial(per_device, mesh.shape["grp"], mesh.shape["rep"]),
        mesh=mesh,
        in_specs=(
            P("pool", "grp"),
            P("rep", "grp"),
            P("rep", "grp"),
            rows,
            P("grp", "rep"),
            P(),
            rows,
            rows,
            P(("grp", "rep"), None, "pool"),
            P(("grp", "rep"), None, "pool"),
            P(("grp", "rep"), "pool", None),
        ),
        out_specs=(rows, rows),
        check_vma=False,
    )
```

```python
import functools
import math

import jax
import jax.numpy as jnp
from jax import lax
from jax.experimental import pallas as pl
from jax.experimental.pallas import tpu as pltpu
from jax.sharding import PartitionSpec as P

HEAD_DIM = 128
CHUNKS = 8
SLOTS = 2
PAIR = CHUNKS * SLOTS
MESH = pl.DeviceIdType.MESH
BF = jnp.bfloat16
F32 = jnp.float32


def remote(src, dst, send, recv, where):
    return pltpu.make_async_remote_copy(
        src_ref=src,
        dst_ref=dst,
        send_sem=send,
        recv_sem=recv,
        device_id=where,
        device_id_type=MESH,
    )


def layer(
    G, R,
    q_hbm, k_hbm, v_hbm, ow_hbm, hidden_ref, gain_ref, routes_ref, weights_ref, wg_hbm, wu_hbm, wd_hbm,
    mid_ref, mix_ref,
    q_s, k_s, v_s, ow_s, wg_s, wu_s, wd_s, load_sem,
    part_s, stat_s, part_r, stat_r, attn_s,
    cols_s, cols_r, sel_s, comb_s,
    disp_s, disp_r, rows_s, act_s, half_s, half_r, sum_s, back_s, back_r,
    part_ss, part_rs, stat_ss, stat_rs, attn_ss, attn_rs,
    cols_ss, cols_rs, disp_ss, disp_rs,
    rows_ss, rows_rs, half_ss, half_rs, back_ss, back_rs,
):
    pool, grp, rep = lax.axis_index("pool"), lax.axis_index("grp"), lax.axis_index("rep")
    E = G * R
    wide = math.isqrt(R)
    me = grp * R + rep
    sibling = (1 - pool, grp, rep)

    way = 1 - 2 * pool
    x, z = rep // wide, rep % wide
    ahead_y = [lax.rem(grp + way * d + G, G) for d in range(G)]
    behind_y = [lax.rem(grp - way * d + G, G) for d in range(G)]
    ahead_x = [lax.rem(x + way * d + wide, wide) * wide for d in range(wide)]
    behind_x = [lax.rem(x - way * d + wide, wide) * wide for d in range(wide)]
    ahead_z = [lax.rem(z + way * d + wide, wide) for d in range(wide)]
    behind_z = [lax.rem(z - way * d + wide, wide) for d in range(wide)]

    def ahead(d):
        d, plane = d % R, d // R
        return ahead_y[plane], ahead_x[d // wide] + ahead_z[d % wide]

    def behind(d):
        d, plane = d % R, d // R
        return behind_y[plane], behind_x[d // wide] + behind_z[d % wide]

    near = [i * (R // 2 - 1) % R for i in range(1, R)]
    far = [i * (E // 2 - 5) % E for i in range(1, E)]

    loads = [
        pltpu.make_async_copy(src, dst, load_sem.at[i])
        for i, (src, dst) in enumerate(
            (
                (q_hbm, q_s),
                (k_hbm, k_s),
                (v_hbm, v_s),
                (ow_hbm, ow_s),
                (wg_hbm, wg_s),
                (wu_hbm, wu_s),
                (wd_hbm, wd_s),
            )
        )
    ]
    for load in loads[:3]:
        load.start()

    barrier = pltpu.get_barrier_semaphore()
    for d in far:
        pl.semaphore_signal(barrier, inc=1, device_id=(pool, *ahead(d)), device_id_type=MESH)
    pl.semaphore_signal(barrier, inc=1, device_id=sibling, device_id_type=MESH)

    lane = lax.broadcasted_iota(jnp.int32, (1, E * PAIR), 1)
    expert, chunk, slot = lane // PAIR, lane % PAIR // SLOTS, lane % SLOTS
    few, topk = routes_ref.shape
    before = jnp.zeros((1, E * PAIR), jnp.int32)
    taken, weights = [], []
    for r in range(few):
        named, weight = jnp.zeros_like(before), jnp.zeros(before.shape, F32)
        for k in range(topk):
            hit = expert == routes_ref[r, k]
            named = jnp.where(hit, 1, named)
            weight = jnp.where(hit, weights_ref[r, k], weight)
        use = jnp.where(before == slot, named, 0).astype(F32)
        taken.append(use)
        weights.append(use * weight)
        before = before + named
    of_row = lax.broadcasted_iota(jnp.int32, (CHUNKS * few, E * PAIR), 0) // few
    select = jnp.where(of_row == chunk, jnp.concatenate(taken * CHUNKS, axis=0), 0.0)
    sel_s[...] = select.T.astype(BF)
    combine = jnp.where(of_row == chunk, jnp.concatenate(weights * CHUNKS, axis=0), 0.0)
    high = combine.astype(BF)
    comb_s[0] = high
    comb_s[1] = (combine - high.astype(F32)).astype(BF)

    for load in loads[:3]:
        load.wait()
    for load in loads[3:]:
        load.start()
    pl.semaphore_wait(barrier, E)

    rows_all, width = q_s.shape
    heads = width // HEAD_DIM
    share = rows_all // R
    lanes = share * heads
    scale = HEAD_DIM ** (-0.5)
    order = R // 2 - 1

    def target(s):
        d = lax.rem((s + 1) * order, R)
        across = lax.rem(x + way * (d // wide) + wide, wide)
        return across * wide + lax.rem(z + way * lax.rem(d, wide) + wide, wide)

    def part_copy(s, peer):
        where = (pool, grp, peer)
        return (
            remote(part_s.at[s], part_r.at[s], part_ss.at[s], part_rs.at[s], where),
            remote(stat_s.at[s], stat_r.at[s], stat_ss.at[s], stat_rs.at[s], where),
        )

    def attend(s):
        peer = target(s)
        block = pl.ds(pl.multiple_of(peer * share, share), share)
        query = jnp.concatenate(
            [q_s[block, h * HEAD_DIM : (h + 1) * HEAD_DIM] for h in range(heads)], axis=0
        )
        scores = lax.dot_general(
            query, k_s[...], (((1,), (1,)), ((), ())), preferred_element_type=F32
        )
        top = jnp.max(scores, axis=1, keepdims=True)
        probs = jnp.exp((scores - top) * scale)
        total = jnp.sum(probs, axis=1, keepdims=True)
        part = jnp.dot(probs.astype(BF), v_s[...], preferred_element_type=F32)
        part_s[s] = part.astype(BF)
        first = lax.broadcasted_iota(jnp.int32, (lanes, 128), 1) < 4
        stat_s[s] = jnp.where(first, top, total).T[:8]

        @pl.when(s < R - 1)
        def _():
            for copy in part_copy(s, peer):
                copy.start()

    unroll = 4

    def attend_some(i, carry):
        for j in range(unroll):
            attend(i * unroll + j)
        return carry

    lax.fori_loop(0, R // unroll, attend_some, 0)
    for s in range(R - 1):
        for copy in part_copy(s, rep):
            copy.wait_recv()

    stats = [stat_r[s] for s in range(R - 1)] + [stat_s[R - 1]]
    top = functools.reduce(jnp.maximum, [stat[0:1] for stat in stats])
    factors = [jnp.exp((stat[0:1] - top) * scale) for stat in stats]
    total = functools.reduce(
        jnp.add, [stat[4:5] * factor for stat, factor in zip(stats, factors)]
    )
    factors = [factor / total for factor in factors]
    factors = jnp.concatenate(factors + [jnp.zeros((128 - R, lanes), F32)], axis=0).T
    weighted = part_s[R - 1].astype(F32) * factors[:, R - 1 : R]
    for s in range(R - 1):
        weighted += part_r[s].astype(F32) * factors[:, s : s + 1]
    attention = weighted.astype(BF)
    mine = pl.ds(pl.multiple_of(rep * share, share), share)
    for h in range(heads):
        attn_s[mine, h * HEAD_DIM : (h + 1) * HEAD_DIM] = attention[h * share : (h + 1) * share]

    def attn_copy(d, block):
        at = attn_s.at[pl.ds(pl.multiple_of(block * share, share), share)]
        return remote(at, at, attn_ss.at[d - 1], attn_rs.at[d - 1], (pool, *ahead(d)))

    for d in near:
        attn_copy(d, rep).start()
    for d in near:
        attn_copy(d, behind(d)[1]).wait_recv()
    loads[3].wait()
    projected = jnp.dot(attn_s[...], ow_s[...], preferred_element_type=F32)
    for e in range(E):
        cols_s[e] = projected[e * few : (e + 1) * few]

    def pair_copy(src, dst, send, recv, d, a, b):
        return remote(
            src.at[a], dst.at[b], send.at[d - 1], recv.at[d - 1], (pool, *ahead(d))
        )

    def cols_copy(d, a, b):
        return pair_copy(cols_s, cols_r, cols_ss, cols_rs, d, a, b)

    def disp_copy(d, a, b):
        return pair_copy(disp_s, disp_r, disp_ss, disp_rs, d, a, b)

    def back_copy(d, a, b):
        return pair_copy(back_s, back_r, back_ss, back_rs, d, a, b)

    def to(d):
        there, along = ahead(d)
        return there * R + along

    def source(d):
        there, along = behind(d)
        return there * R + along

    for d in far:
        cols_copy(d, to(d), me).start()
    cols_r[me] = cols_s[me]
    for d in far:
        cols_copy(d, me, source(d)).wait_recv()
    summed = cols_r[0:R]
    for g in range(1, G):
        summed = summed + cols_r[g * R : (g + 1) * R]
    summed = summed.astype(BF).astype(F32)
    projected = jnp.concatenate([summed[j] for j in range(R)], axis=1)
    mid = (hidden_ref[...].astype(F32) + projected).astype(BF)
    mid_ref[...] = mid
    wider = mid.astype(F32)
    inverse = lax.rsqrt(jnp.mean(wider * wider, axis=-1, keepdims=True) + 1e-06)
    normed = wider * inverse * gain_ref[...].astype(F32).reshape(1, -1)
    piece = normed.shape[1] // CHUNKS
    pieces = jnp.concatenate(
        [normed[:, c * piece : (c + 1) * piece] for c in range(CHUNKS)], axis=0
    ).astype(BF)

    tile = R * PAIR
    for t in range(G):
        chosen = jnp.dot(
            sel_s[t * tile : (t + 1) * tile, :], pieces, preferred_element_type=F32
        )
        disp_s[t * R : (t + 1) * R] = chosen.astype(BF).reshape(R, PAIR, piece)
    for d in far:
        disp_copy(d, to(d), me).start()
    disp_r[me] = disp_s[me]

    row = lax.broadcasted_iota(jnp.int32, (tile, tile), 0)
    col = lax.broadcasted_iota(jnp.int32, (tile, tile), 1)
    pairs = R * SLOTS

    def moved(i):
        return lax.rem(i, pairs) // SLOTS * PAIR + i // pairs * SLOTS + lax.rem(i, SLOTS)

    gather = jnp.where(col == moved(row), 1.0, 0.0).astype(BF)
    spread = jnp.where(row == moved(col), 1.0, 0.0).astype(BF)
    side = E * SLOTS

    def rows_copy(i, half, t):
        at = rows_s.at[pl.ds(pl.multiple_of(half * side + t * pairs, pairs), pairs)]
        return remote(at, at, rows_ss.at[i], rows_rs.at[i], sibling)

    for i in range(G):
        t = behind_y[i]
        for d in range(i * R, (i + 1) * R):
            if d:
                disp_copy(d, me, source(d)).wait_recv()
        arrived = disp_r[pl.ds(t * R, R)].reshape(tile, piece)
        ordered = jnp.dot(gather, arrived, preferred_element_type=F32).astype(BF)
        at = pl.ds(pl.multiple_of(pool * side + t * pairs, pairs), pairs)
        for c in range(CHUNKS):
            rows_s[at, c * piece : (c + 1) * piece] = ordered[c * pairs : (c + 1) * pairs]
        rows_copy(i, pool, t).start()
    for i in range(G):
        rows_copy(i, 1 - pool, ahead_y[i]).wait_recv()
    loads[4].wait()
    loads[5].wait()
    hidden = act_s.shape[1]
    step = min(256, hidden)

    def expand(n, carry):
        at = pl.ds(pl.multiple_of(n * step, step), step)
        gate = jnp.dot(rows_s[...], wg_s[0, :, at], preferred_element_type=F32)
        upper = jnp.dot(rows_s[...], wu_s[0, :, at], preferred_element_type=F32)
        act_s[:, at] = (gate / (1.0 + jnp.exp(-gate)) * upper).astype(BF)
        return carry

    lax.fori_loop(0, hidden // step, expand, 0)
    loads[6].wait()

    def half_copy(n):
        return remote(
            half_s.at[n, 1 - pool], half_r.at[n], half_ss.at[n], half_rs.at[n], sibling
        )

    def contract(n, carry):
        at = pl.ds(pl.multiple_of(n * piece, piece), piece)
        out = jnp.dot(act_s[...], wd_s[0, :, at], preferred_element_type=F32)
        half_s[n, 0] = out[:side].astype(BF)
        half_s[n, 1] = out[side:].astype(BF)
        half_copy(n).start()
        return carry

    lax.fori_loop(0, CHUNKS, contract, 0)
    for n in range(CHUNKS):
        half_copy(n).wait_recv()
        sum_s[n] = (half_s[n, pool].astype(F32) + half_r[n].astype(F32)).astype(BF)
    for t in range(G):
        stacked = sum_s[:, t * pairs : (t + 1) * pairs, :].reshape(tile, piece)
        out = jnp.dot(spread, stacked, preferred_element_type=F32).astype(BF)
        back_s[t * R : (t + 1) * R] = out.reshape(R, PAIR, piece)
    for d in far:
        back_copy(d, to(d), me).start()
    back_r[me] = back_s[me]
    for d in far:
        back_copy(d, me, source(d)).wait_recv()
    returned = back_r[...].reshape(E * PAIR, piece)
    mixed = jnp.dot(comb_s[0], returned, preferred_element_type=F32) + jnp.dot(
        comb_s[1], returned, preferred_element_type=F32
    )
    for c in range(CHUNKS):
        mix_ref[:, c * piece : (c + 1) * piece] = mixed[c * few : (c + 1) * few].astype(BF)

    for s in range(R - 1):
        for copy in part_copy(s, rep):
            copy.wait_send()
    for d in near:
        attn_copy(d, rep).wait_send()
    for d in far:
        cols_copy(d, to(d), me).wait_send()
        disp_copy(d, to(d), me).wait_send()
        back_copy(d, to(d), me).wait_send()
    for i in range(G):
        rows_copy(i, pool, behind_y[i]).wait_send()
    for n in range(CHUNKS):
        half_copy(n).wait_send()


def per_device(
    G, R,
    queries, keys, values, hidden_in, o_weight, norm_gain, routes, route_weights,
    w_gate, w_up, w_down,
):
    E = G * R
    rows_all, width = queries.shape
    few, model = hidden_in.shape
    block = o_weight.shape[1]
    hidden = w_gate.shape[2]
    heads = width // HEAD_DIM
    share = rows_all // R
    lanes = share * heads
    piece = model // CHUNKS
    side = E * SLOTS

    vmem = pl.BlockSpec(memory_space=pltpu.VMEM)
    smem = pl.BlockSpec(memory_space=pltpu.SMEM)
    anywhere = pl.BlockSpec(memory_space=pl.ANY)
    dma = pltpu.SemaphoreType.DMA
    scratch = [
        pltpu.VMEM(queries.shape, BF),
        pltpu.VMEM(keys.shape, BF),
        pltpu.VMEM(values.shape, BF),
        pltpu.VMEM(o_weight.shape, BF),
        pltpu.VMEM(w_gate.shape, BF),
        pltpu.VMEM(w_up.shape, BF),
        pltpu.VMEM(w_down.shape, BF),
        dma((7,)),
        pltpu.VMEM((R, lanes, HEAD_DIM), BF),
        pltpu.VMEM((R, 8, lanes), F32),
        pltpu.VMEM((R - 1, lanes, HEAD_DIM), BF),
        pltpu.VMEM((R - 1, 8, lanes), F32),
        pltpu.VMEM((rows_all, width), BF),
        pltpu.VMEM((E, few, block), F32),
        pltpu.VMEM((E, few, block), F32),
        pltpu.VMEM((E * PAIR, CHUNKS * few), BF),
        pltpu.VMEM((2, CHUNKS * few, E * PAIR), BF),
        pltpu.VMEM((E, PAIR, piece), BF),
        pltpu.VMEM((E, PAIR, piece), BF),
        pltpu.VMEM((2 * side, model), BF),
        pltpu.VMEM((2 * side, hidden), BF),
        pltpu.VMEM((CHUNKS, 2, side, piece), BF),
        pltpu.VMEM((CHUNKS, side, piece), BF),
        pltpu.VMEM((CHUNKS, side, piece), BF),
        pltpu.VMEM((E, PAIR, piece), BF),
        pltpu.VMEM((E, PAIR, piece), BF),
    ]
    for count in (R - 1, R - 1, R - 1, E - 1, E - 1, G, CHUNKS, E - 1):
        scratch += [dma((count,)), dma((count,))]
    return pl.pallas_call(
        functools.partial(layer, G, R),
        out_shape=[jax.ShapeDtypeStruct(hidden_in.shape, BF)] * 2,
        in_specs=[anywhere] * 4 + [vmem] * 2 + [smem] * 2 + [anywhere] * 3,
        out_specs=[vmem] * 2,
        scratch_shapes=scratch,
        compiler_params=pltpu.CompilerParams(
            collective_id=0, has_side_effects=True, vmem_limit_bytes=58 << 20
        ),
        name="decode_layer",
    )(
        queries, keys, values, o_weight,
        hidden_in, norm_gain, routes, route_weights,
        w_gate, w_up, w_down,
    )


def solution(mesh):
    rows = P(("pool", "grp", "rep"), None)
    return jax.shard_map(
        functools.partial(per_device, mesh.shape["grp"], mesh.shape["rep"]),
        mesh=mesh,
        in_specs=(
            P("pool", "grp"),
            P("rep", "grp"),
            P("rep", "grp"),
            rows,
            P("grp", "rep"),
            P(),
            rows,
            rows,
            P(("grp", "rep"), None, "pool"),
            P(("grp", "rep"), None, "pool"),
            P(("grp", "rep"), "pool", None),
        ),
        out_specs=(rows, rows),
        check_vma=False,
    )
```

```python
import functools
import math

import jax
import jax.numpy as jnp
from jax import lax
from jax.experimental import pallas as pl
from jax.experimental.pallas import tpu as pltpu
from jax.sharding import PartitionSpec as P

HEAD_DIM = 128
CHUNKS = 8
SLOTS = 2
PAIR = CHUNKS * SLOTS
MESH = pl.DeviceIdType.MESH
BF = jnp.bfloat16
F32 = jnp.float32


def remote(src, dst, send, recv, where):
    return pltpu.make_async_remote_copy(
        src_ref=src,
        dst_ref=dst,
        send_sem=send,
        recv_sem=recv,
        device_id=where,
        device_id_type=MESH,
    )


def layer(
    G, R,
    q_hbm, k_hbm, v_hbm, ow_hbm, hidden_ref, gain_ref, routes_ref, weights_ref, wg_hbm, wu_hbm, wd_hbm,
    mid_ref, mix_ref,
    q_s, k_s, v_s, ow_s, wg_s, wu_s, wd_s, load_sem,
    part_s, stat_s, part_r, stat_r, attn_s,
    cols_s, cols_r, sel_s, comb_s, perm_s,
    disp_s, disp_r, rows_s, act_s, half_s, half_r, sum_s, back_s, back_r,
    part_ss, part_rs, stat_ss, stat_rs, attn_ss, attn_rs,
    cols_ss, cols_rs, disp_ss, disp_rs,
    rows_ss, rows_rs, half_ss, half_rs, back_ss, back_rs,
):
    pool, grp, rep = lax.axis_index("pool"), lax.axis_index("grp"), lax.axis_index("rep")
    E = G * R
    wide = math.isqrt(R)
    me = grp * R + rep
    sibling = (1 - pool, grp, rep)

    way = 1 - 2 * pool
    x, z = rep // wide, rep % wide
    ahead_y = [lax.rem(grp + way * d + G, G) for d in range(G)]
    behind_y = [lax.rem(grp - way * d + G, G) for d in range(G)]
    ahead_x = [lax.rem(x + way * d + wide, wide) * wide for d in range(wide)]
    behind_x = [lax.rem(x - way * d + wide, wide) * wide for d in range(wide)]
    ahead_z = [lax.rem(z + way * d + wide, wide) for d in range(wide)]
    behind_z = [lax.rem(z - way * d + wide, wide) for d in range(wide)]

    def ahead(d):
        d, plane = d % R, d // R
        return ahead_y[plane], ahead_x[d // wide] + ahead_z[d % wide]

    def behind(d):
        d, plane = d % R, d // R
        return behind_y[plane], behind_x[d // wide] + behind_z[d % wide]

    near = [i * (R // 2 - 1) % R for i in range(1, R)]
    far = [i * (E // 2 - 5) % E for i in range(1, E)]

    loads = [
        pltpu.make_async_copy(src, dst, load_sem.at[i])
        for i, (src, dst) in enumerate(
            (
                (q_hbm, q_s),
                (k_hbm, k_s),
                (v_hbm, v_s),
                (ow_hbm, ow_s),
                (wg_hbm, wg_s),
                (wu_hbm, wu_s),
                (wd_hbm, wd_s),
            )
        )
    ]
    for load in loads[:3]:
        load.start()

    barrier = pltpu.get_barrier_semaphore()
    for d in far:
        pl.semaphore_signal(barrier, inc=1, device_id=(pool, *ahead(d)), device_id_type=MESH)
    pl.semaphore_signal(barrier, inc=1, device_id=sibling, device_id_type=MESH)

    for load in loads[:3]:
        load.wait()
    loads[3].start()

    rows_all, width = q_s.shape
    heads = width // HEAD_DIM
    share = rows_all // R
    lanes = share * heads
    scale = HEAD_DIM ** (-0.5)
    order = R // 2 - 1

    def target(s):
        d = lax.rem((s + 1) * order, R)
        across = lax.rem(x + way * (d // wide) + wide, wide)
        return across * wide + lax.rem(z + way * lax.rem(d, wide) + wide, wide)

    def part_copy(s, peer):
        where = (pool, grp, peer)
        return (
            remote(part_s.at[s], part_r.at[s], part_ss.at[s], part_rs.at[s], where),
            remote(stat_s.at[s], stat_r.at[s], stat_ss.at[s], stat_rs.at[s], where),
        )

    def attend(s):
        peer = target(s)
        block = pl.ds(pl.multiple_of(peer * share, share), share)
        query = jnp.concatenate(
            [q_s[block, h * HEAD_DIM : (h + 1) * HEAD_DIM] for h in range(heads)], axis=0
        )
        scores = lax.dot_general(
            query, k_s[...], (((1,), (1,)), ((), ())), preferred_element_type=F32
        )
        top = jnp.max(scores, axis=1, keepdims=True)
        probs = jnp.exp((scores - top) * scale)
        total = jnp.sum(probs, axis=1, keepdims=True)
        part = jnp.dot(probs.astype(BF), v_s[...], preferred_element_type=F32)
        part_s[s] = part.astype(BF)
        first = lax.broadcasted_iota(jnp.int32, (lanes, 128), 1) < 4
        stat_s[s] = jnp.where(first, top, total).T[:8]

    unroll = 4

    def attend_some(i, carry):
        for j in range(unroll):
            s = i * unroll + j
            attend(s)

            @pl.when(s < R - 1)
            def _():
                for copy in part_copy(s, target(s)):
                    copy.start()

        return carry

    few, topk = routes_ref.shape
    for s in range(unroll):
        attend(s)
    pl.semaphore_wait(barrier, E)
    for s in range(min(unroll, R - 1)):
        for copy in part_copy(s, target(s)):
            copy.start()
    lax.fori_loop(1, R // unroll, attend_some, 0)
    for s in range(R - 1):
        for copy in part_copy(s, rep):
            copy.wait_recv()

    stats = [stat_r[s] for s in range(R - 1)] + [stat_s[R - 1]]
    top = functools.reduce(jnp.maximum, [stat[0:1] for stat in stats])
    factors = [jnp.exp((stat[0:1] - top) * scale) for stat in stats]
    total = functools.reduce(
        jnp.add, [stat[4:5] * factor for stat, factor in zip(stats, factors)]
    )
    factors = [factor / total for factor in factors]
    factors = jnp.concatenate(factors + [jnp.zeros((128 - R, lanes), F32)], axis=0).T
    weighted = part_s[R - 1].astype(F32) * factors[:, R - 1 : R]
    for s in range(R - 1):
        weighted += part_r[s].astype(F32) * factors[:, s : s + 1]
    attention = weighted.astype(BF)
    mine = pl.ds(pl.multiple_of(rep * share, share), share)
    for h in range(heads):
        attn_s[mine, h * HEAD_DIM : (h + 1) * HEAD_DIM] = attention[h * share : (h + 1) * share]

    def attn_copy(d, block):
        at = attn_s.at[pl.ds(pl.multiple_of(block * share, share), share)]
        return remote(at, at, attn_ss.at[d - 1], attn_rs.at[d - 1], (pool, *ahead(d)))

    for d in near:
        attn_copy(d, rep).start()
    for load in loads[4:]:
        load.start()

    lane = lax.broadcasted_iota(jnp.int32, (1, E * PAIR), 1)
    expert, chunk, slot = lane // PAIR, lane % PAIR // SLOTS, lane % SLOTS
    before = jnp.zeros((1, E * PAIR), jnp.int32)
    taken, weights = [], []
    for r in range(few):
        named, weight = jnp.zeros_like(before), jnp.zeros(before.shape, F32)
        for k in range(topk):
            hit = expert == routes_ref[r, k]
            named = jnp.where(hit, 1, named)
            weight = jnp.where(hit, weights_ref[r, k], weight)
        use = jnp.where(before == slot, named, 0).astype(F32)
        taken.append(use)
        weights.append(use * weight)
        before = before + named
    of_row = lax.broadcasted_iota(jnp.int32, (CHUNKS * few, E * PAIR), 0) // few
    select = jnp.where(of_row == chunk, jnp.concatenate(taken * CHUNKS, axis=0), 0.0)
    sel_s[...] = select.T.astype(BF)
    combine = jnp.where(of_row == chunk, jnp.concatenate(weights * CHUNKS, axis=0), 0.0)
    high = combine.astype(BF)
    comb_s[0] = high
    comb_s[1] = (combine - high.astype(F32)).astype(BF)

    tile = R * PAIR
    pairs = R * SLOTS
    row = lax.broadcasted_iota(jnp.int32, (tile, tile), 0)
    col = lax.broadcasted_iota(jnp.int32, (tile, tile), 1)

    def moved(i):
        return lax.rem(i, pairs) // SLOTS * PAIR + i // pairs * SLOTS + lax.rem(i, SLOTS)

    perm_s[0] = jnp.where(col == moved(row), 1.0, 0.0).astype(BF)
    perm_s[1] = jnp.where(row == moved(col), 1.0, 0.0).astype(BF)

    for d in near:
        attn_copy(d, behind(d)[1]).wait_recv()
    loads[3].wait()
    projected = jnp.dot(attn_s[...], ow_s[...], preferred_element_type=F32)
    for e in range(E):
        cols_s[e] = projected[e * few : (e + 1) * few]

    def pair_copy(src, dst, send, recv, d, a, b):
        return remote(
            src.at[a], dst.at[b], send.at[d - 1], recv.at[d - 1], (pool, *ahead(d))
        )

    def cols_copy(d, a, b):
        return pair_copy(cols_s, cols_r, cols_ss, cols_rs, d, a, b)

    def disp_copy(d, a, b):
        return pair_copy(disp_s, disp_r, disp_ss, disp_rs, d, a, b)

    def back_copy(d, a, b):
        return pair_copy(back_s, back_r, back_ss, back_rs, d, a, b)

    def to(d):
        there, along = ahead(d)
        return there * R + along

    def source(d):
        there, along = behind(d)
        return there * R + along

    for d in far:
        cols_copy(d, to(d), me).start()
    cols_r[me] = cols_s[me]
    for d in far:
        cols_copy(d, me, source(d)).wait_recv()
    summed = cols_r[0:R]
    for g in range(1, G):
        summed = summed + cols_r[g * R : (g + 1) * R]
    summed = summed.astype(BF).astype(F32)
    projected = jnp.concatenate([summed[j] for j in range(R)], axis=1)
    mid = (hidden_ref[...].astype(F32) + projected).astype(BF)
    mid_ref[...] = mid
    wider = mid.astype(F32)
    inverse = lax.rsqrt(jnp.mean(wider * wider, axis=-1, keepdims=True) + 1e-06)
    normed = wider * inverse * gain_ref[...].astype(F32).reshape(1, -1)
    piece = normed.shape[1] // CHUNKS
    pieces = jnp.concatenate(
        [normed[:, c * piece : (c + 1) * piece] for c in range(CHUNKS)], axis=0
    ).astype(BF)

    planes = G // 2
    groups = [range(j * planes, (j + 1) * planes) for j in range(2)]

    def sent(j, sign):
        return [d for d in far if sign * (d // R) % G in groups[j]]

    for j in range(2):
        for i in groups[j]:
            t = ahead_y[i]
            chosen = jnp.dot(
                sel_s[pl.ds(pl.multiple_of(t * tile, tile), tile), :],
                pieces,
                preferred_element_type=F32,
            )
            disp_s[pl.ds(t * R, R)] = chosen.astype(BF).reshape(R, PAIR, piece)
        for d in sent(j, 1):
            disp_copy(d, to(d), me).start()
    disp_r[me] = disp_s[me]
    half = planes * pairs

    def rows_copy(i, of):
        at = rows_s.at[i // planes, pl.ds(of * half + i % planes * pairs, pairs)]
        return remote(at, at, rows_ss.at[i], rows_rs.at[i], sibling)

    def collect(j):
        for i in groups[j]:
            for d in range(i * R, (i + 1) * R):
                if d:
                    disp_copy(d, me, source(d)).wait_recv()
            arrived = disp_r[pl.ds(behind_y[i] * R, R)].reshape(tile, piece)
            ordered = jnp.dot(perm_s[0], arrived, preferred_element_type=F32).astype(BF)
            at = pl.ds(pl.multiple_of(pool * half + i % planes * pairs, pairs), pairs)
            for c in range(CHUNKS):
                rows_s[j, at, c * piece : (c + 1) * piece] = ordered[c * pairs : (c + 1) * pairs]
            rows_copy(i, pool).start()

    hidden = act_s.shape[1]
    step = min(256, hidden)

    def half_copy(j, n):
        return remote(
            half_s.at[j, n, 1 - pool], half_r.at[j, n], half_ss.at[j, n], half_rs.at[j, n], sibling
        )

    def apply(j):
        for i in groups[j]:
            rows_copy(i, 1 - pool).wait_recv()
        if j == 0:
            loads[4].wait()
            loads[5].wait()

        def expand(n, carry):
            at = pl.ds(pl.multiple_of(n * step, step), step)
            gate = jnp.dot(rows_s[j], wg_s[0, :, at], preferred_element_type=F32)
            upper = jnp.dot(rows_s[j], wu_s[0, :, at], preferred_element_type=F32)
            act_s[:, at] = (gate / (1.0 + jnp.exp(-gate)) * upper).astype(BF)
            return carry

        lax.fori_loop(0, hidden // step, expand, 0)
        if j == 0:
            loads[6].wait()

        def contract(n, carry):
            at = pl.ds(pl.multiple_of(n * piece, piece), piece)
            out = jnp.dot(act_s[...], wd_s[0, :, at], preferred_element_type=F32)
            half_s[j, n, 0] = out[:half].astype(BF)
            half_s[j, n, 1] = out[half:].astype(BF)
            half_copy(j, n).start()
            return carry

        lax.fori_loop(0, CHUNKS, contract, 0)

    def give_back(j):
        for n in range(CHUNKS):
            half_copy(j, n).wait_recv()
            sum_s[n] = (half_s[j, n, pool].astype(F32) + half_r[j, n].astype(F32)).astype(BF)
        for i in groups[j]:
            k = i % planes * pairs
            stacked = sum_s[:, k : k + pairs, :].reshape(tile, piece)
            out = jnp.dot(perm_s[1], stacked, preferred_element_type=F32).astype(BF)
            back_s[pl.ds(behind_y[i] * R, R)] = out.reshape(R, PAIR, piece)
        for d in sent(j, -1):
            back_copy(d, to(d), me).start()

    collect(0)
    apply(0)
    collect(1)
    give_back(0)
    apply(1)
    give_back(1)
    back_r[me] = back_s[me]
    for d in far:
        back_copy(d, me, source(d)).wait_recv()
    returned = back_r[...].reshape(E * PAIR, piece)
    mixed = jnp.dot(comb_s[0], returned, preferred_element_type=F32) + jnp.dot(
        comb_s[1], returned, preferred_element_type=F32
    )
    for c in range(CHUNKS):
        mix_ref[:, c * piece : (c + 1) * piece] = mixed[c * few : (c + 1) * few].astype(BF)

    for s in range(R - 1):
        for copy in part_copy(s, rep):
            copy.wait_send()
    for d in near:
        attn_copy(d, rep).wait_send()
    for d in far:
        cols_copy(d, to(d), me).wait_send()
        disp_copy(d, to(d), me).wait_send()
        back_copy(d, to(d), me).wait_send()
    for i in range(G):
        rows_copy(i, pool).wait_send()
    for j in range(2):
        for n in range(CHUNKS):
            half_copy(j, n).wait_send()


def per_device(
    G, R,
    queries, keys, values, hidden_in, o_weight, norm_gain, routes, route_weights,
    w_gate, w_up, w_down,
):
    E = G * R
    rows_all, width = queries.shape
    few, model = hidden_in.shape
    block = o_weight.shape[1]
    hidden = w_gate.shape[2]
    heads = width // HEAD_DIM
    share = rows_all // R
    lanes = share * heads
    piece = model // CHUNKS
    side = E * SLOTS

    vmem = pl.BlockSpec(memory_space=pltpu.VMEM)
    smem = pl.BlockSpec(memory_space=pltpu.SMEM)
    anywhere = pl.BlockSpec(memory_space=pl.ANY)
    dma = pltpu.SemaphoreType.DMA
    scratch = [
        pltpu.VMEM(queries.shape, BF),
        pltpu.VMEM(keys.shape, BF),
        pltpu.VMEM(values.shape, BF),
        pltpu.VMEM(o_weight.shape, BF),
        pltpu.VMEM(w_gate.shape, BF),
        pltpu.VMEM(w_up.shape, BF),
        pltpu.VMEM(w_down.shape, BF),
        dma((7,)),
        pltpu.VMEM((R, lanes, HEAD_DIM), BF),
        pltpu.VMEM((R, 8, lanes), F32),
        pltpu.VMEM((R - 1, lanes, HEAD_DIM), BF),
        pltpu.VMEM((R - 1, 8, lanes), F32),
        pltpu.VMEM((rows_all, width), BF),
        pltpu.VMEM((E, few, block), F32),
        pltpu.VMEM((E, few, block), F32),
        pltpu.VMEM((E * PAIR, CHUNKS * few), BF),
        pltpu.VMEM((2, CHUNKS * few, E * PAIR), BF),
        pltpu.VMEM((2, R * PAIR, R * PAIR), BF),
        pltpu.VMEM((E, PAIR, piece), BF),
        pltpu.VMEM((E, PAIR, piece), BF),
        pltpu.VMEM((2, side, model), BF),
        pltpu.VMEM((side, hidden), BF),
        pltpu.VMEM((2, CHUNKS, 2, side // 2, piece), BF),
        pltpu.VMEM((2, CHUNKS, side // 2, piece), BF),
        pltpu.VMEM((CHUNKS, side // 2, piece), BF),
        pltpu.VMEM((E, PAIR, piece), BF),
        pltpu.VMEM((E, PAIR, piece), BF),
    ]
    for count in (R - 1, R - 1, R - 1, E - 1, E - 1, G, (2, CHUNKS), E - 1):
        shape = count if isinstance(count, tuple) else (count,)
        scratch += [dma(shape), dma(shape)]
    return pl.pallas_call(
        functools.partial(layer, G, R),
        out_shape=[jax.ShapeDtypeStruct(hidden_in.shape, BF)] * 2,
        in_specs=[anywhere] * 4 + [vmem] * 2 + [smem] * 2 + [anywhere] * 3,
        out_specs=[vmem] * 2,
        scratch_shapes=scratch,
        compiler_params=pltpu.CompilerParams(
            collective_id=0, has_side_effects=True, vmem_limit_bytes=58 << 20
        ),
        name="decode_layer",
    )(
        queries, keys, values, o_weight,
        hidden_in, norm_gain, routes, route_weights,
        w_gate, w_up, w_down,
    )


def solution(mesh):
    rows = P(("pool", "grp", "rep"), None)
    return jax.shard_map(
        functools.partial(per_device, mesh.shape["grp"], mesh.shape["rep"]),
        mesh=mesh,
        in_specs=(
            P("pool", "grp"),
            P("rep", "grp"),
            P("rep", "grp"),
            rows,
            P("grp", "rep"),
            P(),
            rows,
            rows,
            P(("grp", "rep"), None, "pool"),
            P(("grp", "rep"), None, "pool"),
            P(("grp", "rep"), "pool", None),
        ),
        out_specs=(rows, rows),
        check_vma=False,
    )
```

```python
import functools
import math

import jax
import jax.numpy as jnp
from jax import lax
from jax.experimental import pallas as pl
from jax.experimental.pallas import tpu as pltpu
from jax.sharding import PartitionSpec as P

HEAD_DIM = 128
CHUNKS = 8
SLOTS = 2
PAIR = CHUNKS * SLOTS
MESH = pl.DeviceIdType.MESH
BF = jnp.bfloat16
F32 = jnp.float32


def remote(src, dst, send, recv, where):
    return pltpu.make_async_remote_copy(
        src_ref=src,
        dst_ref=dst,
        send_sem=send,
        recv_sem=recv,
        device_id=where,
        device_id_type=MESH,
    )


def layer(
    G, R,
    q_hbm, k_hbm, v_hbm, ow_hbm, hidden_ref, gain_ref, routes_ref, weights_ref, wg_hbm, wu_hbm, wd_hbm,
    mid_ref, mix_ref,
    q_s, k_s, v_s, ow_s, wg_s, wu_s, wd_s, load_sem,
    known, part_s, stat_s, part_r, stat_r, next_s, tops_s, next_r, tops_r, attn_s,
    cols_s, cols_r, sel_s, comb_s, perm_s,
    disp_s, disp_r, rows_s, act_s, half_s, half_r, sum_s, back_s, back_r,
    part_ss, part_rs, stat_ss, stat_rs, next_ss, next_rs, tops_ss, tops_rs,
    pass_ss, pass_rs, wide_ss, wide_rs,
    cols_ss, cols_rs, disp_ss, disp_rs,
    rows_ss, rows_rs, half_ss, half_rs, back_ss, back_rs,
):
    pool, grp, rep = lax.axis_index("pool"), lax.axis_index("grp"), lax.axis_index("rep")
    E = G * R
    wide = math.isqrt(R)
    me = grp * R + rep
    sibling = (1 - pool, grp, rep)

    way = 1 - 2 * pool
    x, z = rep // wide, rep % wide
    ahead_y = [lax.rem(grp + way * d + G, G) for d in range(G)]
    behind_y = [lax.rem(grp - way * d + G, G) for d in range(G)]
    ahead_x = [lax.rem(x + way * d + wide, wide) * wide for d in range(wide)]
    behind_x = [lax.rem(x - way * d + wide, wide) * wide for d in range(wide)]
    ahead_z = [lax.rem(z + way * d + wide, wide) for d in range(wide)]
    behind_z = [lax.rem(z - way * d + wide, wide) for d in range(wide)]

    def ahead(d):
        d, plane = d % R, d // R
        return ahead_y[plane], ahead_x[d // wide] + ahead_z[d % wide]

    def behind(d):
        d, plane = d % R, d // R
        return behind_y[plane], behind_x[d // wide] + behind_z[d % wide]

    far = [i * (E // 2 - 5) % E for i in range(1, E)]

    loads = [
        pltpu.make_async_copy(src, dst, load_sem.at[i])
        for i, (src, dst) in enumerate(
            (
                (q_hbm, q_s),
                (k_hbm, k_s),
                (v_hbm, v_s),
                (ow_hbm, ow_s),
                (wg_hbm, wg_s),
                (wu_hbm, wu_s),
                (wd_hbm, wd_s),
            )
        )
    ]
    for load in loads[:3]:
        load.start()

    barrier = pltpu.get_barrier_semaphore()
    along_x = [d * wide for d in range(1, wide)]
    along_z = list(range(1, wide))
    along_y = [d * R for d in range(1, G)]
    axes = along_x + along_z + along_y

    def greet(sem, shifts):
        for d in shifts:
            pl.semaphore_signal(sem, inc=1, device_id=(pool, *ahead(d)), device_id_type=MESH)

    greet(barrier, axes)
    pl.semaphore_signal(barrier, inc=1, device_id=sibling, device_id_type=MESH)

    for load in loads[:3]:
        load.wait()
    loads[3].start()

    rows_all, width = q_s.shape
    heads = width // HEAD_DIM // 2
    share = rows_all // R
    lanes = share * heads
    scale = HEAD_DIM ** (-0.5)
    few, topk = routes_ref.shape
    firsts, seconds = (along_x, along_z), (along_z, along_x)
    across = ([x * wide for x in range(wide)], list(range(wide)))
    orders = [*range(2, wide), 1, 0] if wide > 2 else [1, 0]
    here = (x, z)

    def part_copy(h, k):
        where = (pool, *ahead(firsts[h][k - 1]))
        return [
            remote(a.at[h, k], b.at[h, k - 1], c.at[h, k - 1], d.at[h, k - 1], where)
            for a, b, c, d in ((part_s, part_r, part_ss, part_rs), (stat_s, stat_r, stat_ss, stat_rs))
        ]

    def attend(h, k):
        start = ahead_x[k] if h == 0 else ahead_z[k]
        for pair in range(0, wide, 2):
            pieces = []
            for other in (pair, pair + 1):
                row = pl.multiple_of((start + across[1 - h][other]) * share, share)
                for head in range(h * heads, (h + 1) * heads):
                    pieces.append(
                        q_s[pl.ds(row, share), head * HEAD_DIM : (head + 1) * HEAD_DIM]
                    )
            query = jnp.concatenate(pieces, axis=0)
            scores = lax.dot_general(
                query, k_s[...], (((1,), (1,)), ((), ())), preferred_element_type=F32
            )
            top = jnp.max(scores, axis=1, keepdims=True)
            probs = jnp.exp((scores - top) * scale)
            total = jnp.sum(probs, axis=1, keepdims=True)
            part = jnp.dot(probs.astype(BF), v_s[...], preferred_element_type=F32)
            part_s[h, k, pair * lanes : (pair + 2) * lanes] = part.astype(BF)
            first = lax.broadcasted_iota(jnp.int32, (2 * lanes, 128), 1) < 4
            stat_s[h, k, :, pair * lanes : (pair + 2) * lanes] = (
                jnp.where(first, top, total).T[:8]
            )

    met = False
    for k in orders:
        for h in range(2):
            attend(h, k)
            if not met:
                pl.semaphore_wait(barrier, len(axes) + 1)
                greet(known.at[0], along_x)
                met = True
            if k:
                for copy in part_copy(h, k):
                    copy.start()

    def merged(parts, stats, divide):
        top = functools.reduce(jnp.maximum, [stat[0:1] for stat in stats])
        factors = [jnp.exp((stat[0:1] - top) * scale) for stat in stats]
        total = functools.reduce(
            jnp.add, [stat[4:5] * factor for stat, factor in zip(stats, factors)]
        )
        if divide:
            factors = [factor / total for factor in factors]
        empty = jnp.zeros((128 - len(stats), top.shape[1]), F32)
        columns = jnp.concatenate(factors + [empty], axis=0).T
        out = functools.reduce(
            jnp.add, [part.astype(F32) * columns[:, i : i + 1] for i, part in enumerate(parts)]
        )
        return out.astype(BF), top, total

    def next_copy(h, k):
        d = seconds[h][k - 1]
        there = (ahead_z[k] if h == 0 else ahead_x[k] // wide)
        where = (pool, *ahead(d))
        return [
            remote(a.at[h, there], b.at[h, k - 1], c.at[h, k - 1], d.at[h, k - 1], where)
            for a, b, c, d in ((next_s, next_r, next_ss, next_rs), (tops_s, tops_r, tops_ss, tops_rs))
        ]

    for h in range(2):
        for k in range(1, wide):
            for copy in part_copy(h, k):
                copy.wait_recv()
        out, top, total = merged(
            [part_s[h, 0]] + [part_r[h, k] for k in range(wide - 1)],
            [stat_s[h, 0]] + [stat_r[h, k] for k in range(wide - 1)],
            False,
        )
        first = lax.broadcasted_iota(jnp.int32, (8, lanes), 0) < 4
        for other in range(wide):
            at = slice(other * lanes, (other + 1) * lanes)
            next_s[h, other] = out[at]
            tops_s[h, other] = jnp.where(first, top[:, at], total[:, at])
        for k in range(1, wide):
            for copy in next_copy(h, k):
                copy.start()
    pl.semaphore_wait(known.at[0], wide - 1)
    greet(known.at[1], along_y)

    def pass_copy(h, k, block):
        at = attn_s.at[h, here[h], block]
        where = (pool, *ahead(seconds[h][k - 1]))
        return remote(at, at, pass_ss.at[h, k - 1], pass_rs.at[h, k - 1], where)

    def wide_copy(h, k, block):
        at = attn_s.at[h, block]
        where = (pool, *ahead(firsts[h][k - 1]))
        return remote(at, at, wide_ss.at[h, k - 1], wide_rs.at[h, k - 1], where)

    behind_of = (behind_z, [v // wide for v in behind_x])
    for h in range(2):
        for k in range(1, wide):
            for copy in next_copy(h, k):
                copy.wait_recv()
        mine = here[1 - h]
        out, _, _ = merged(
            [next_s[h, mine]] + [next_r[h, k] for k in range(wide - 1)],
            [tops_s[h, mine]] + [tops_r[h, k] for k in range(wide - 1)],
            True,
        )
        for head in range(heads):
            attn_s[h, here[h], mine, :, head * HEAD_DIM : (head + 1) * HEAD_DIM] = out[
                head * share : (head + 1) * share
            ]
        for k in range(1, wide):
            pass_copy(h, k, mine).start()
    for load in loads[4:]:
        load.start()

    lane = lax.broadcasted_iota(jnp.int32, (1, E * PAIR), 1)
    expert, chunk, slot = lane // PAIR, lane % PAIR // SLOTS, lane % SLOTS
    before = jnp.zeros((1, E * PAIR), jnp.int32)
    taken, weights = [], []
    for r in range(few):
        named, weight = jnp.zeros_like(before), jnp.zeros(before.shape, F32)
        for k in range(topk):
            hit = expert == routes_ref[r, k]
            named = jnp.where(hit, 1, named)
            weight = jnp.where(hit, weights_ref[r, k], weight)
        use = jnp.where(before == slot, named, 0).astype(F32)
        taken.append(use)
        weights.append(use * weight)
        before = before + named
    of_row = lax.broadcasted_iota(jnp.int32, (CHUNKS * few, E * PAIR), 0) // few
    select = jnp.where(of_row == chunk, jnp.concatenate(taken * CHUNKS, axis=0), 0.0)
    sel_s[...] = select.T.astype(BF)
    combine = jnp.where(of_row == chunk, jnp.concatenate(weights * CHUNKS, axis=0), 0.0)
    high = combine.astype(BF)
    comb_s[0] = high
    comb_s[1] = (combine - high.astype(F32)).astype(BF)

    tile = R * PAIR
    pairs = R * SLOTS
    row = lax.broadcasted_iota(jnp.int32, (tile, tile), 0)
    col = lax.broadcasted_iota(jnp.int32, (tile, tile), 1)

    def moved(i):
        return lax.rem(i, pairs) // SLOTS * PAIR + i // pairs * SLOTS + lax.rem(i, SLOTS)

    perm_s[0] = jnp.where(col == moved(row), 1.0, 0.0).astype(BF)
    perm_s[1] = jnp.where(row == moved(col), 1.0, 0.0).astype(BF)

    for h in range(2):
        for k in range(1, wide):
            pass_copy(h, k, behind_of[h][k]).wait_recv()
        for k in range(1, wide):
            wide_copy(h, k, here[h]).start()
    for h in range(2):
        for k in range(1, wide):
            wide_copy(h, k, behind_of[1 - h][k]).wait_recv()
    loads[3].wait()
    middle = width // 2
    straight, turned = [
        jnp.dot(
            attn_s[h].reshape(rows_all, middle),
            ow_s[h * middle : (h + 1) * middle, :],
            preferred_element_type=F32,
        )
        for h in range(2)
    ]
    for e in range(E):
        at = e * few
        block = at // share
        other = (block % wide * wide + block // wide) * share + at % share
        cols_s[e] = straight[at : at + few] + turned[other : other + few]
    pl.semaphore_wait(known.at[1], G - 1)

    def pair_copy(src, dst, send, recv, d, a, b):
        return remote(
            src.at[a], dst.at[b], send.at[d - 1], recv.at[d - 1], (pool, *ahead(d))
        )

    def cols_copy(d, a, b):
        return pair_copy(cols_s, cols_r, cols_ss, cols_rs, d, a, b)

    def disp_copy(d, a, b):
        return pair_copy(disp_s, disp_r, disp_ss, disp_rs, d, a, b)

    def back_copy(d, a, b):
        return pair_copy(back_s, back_r, back_ss, back_rs, d, a, b)

    def to(d):
        there, along = ahead(d)
        return there * R + along

    def source(d):
        there, along = behind(d)
        return there * R + along

    for d in far:
        cols_copy(d, to(d), me).start()
    cols_r[me] = cols_s[me]
    for d in far:
        cols_copy(d, me, source(d)).wait_recv()
    summed = cols_r[0:R]
    for g in range(1, G):
        summed = summed + cols_r[g * R : (g + 1) * R]
    summed = summed.astype(BF).astype(F32)
    projected = jnp.concatenate([summed[j] for j in range(R)], axis=1)
    mid = (hidden_ref[...].astype(F32) + projected).astype(BF)
    mid_ref[...] = mid
    wider = mid.astype(F32)
    inverse = lax.rsqrt(jnp.mean(wider * wider, axis=-1, keepdims=True) + 1e-06)
    normed = wider * inverse * gain_ref[...].astype(F32).reshape(1, -1)
    piece = normed.shape[1] // CHUNKS
    pieces = jnp.concatenate(
        [normed[:, c * piece : (c + 1) * piece] for c in range(CHUNKS)], axis=0
    ).astype(BF)

    planes = G // 2
    groups = [range(j * planes, (j + 1) * planes) for j in range(2)]

    def sent(j, sign):
        return [d for d in far if sign * (d // R) % G in groups[j]]

    for j in range(2):
        for i in groups[j]:
            t = ahead_y[i]
            chosen = jnp.dot(
                sel_s[pl.ds(pl.multiple_of(t * tile, tile), tile), :],
                pieces,
                preferred_element_type=F32,
            )
            disp_s[pl.ds(t * R, R)] = chosen.astype(BF).reshape(R, PAIR, piece)
        for d in sent(j, 1):
            disp_copy(d, to(d), me).start()
    disp_r[me] = disp_s[me]
    half = planes * pairs

    def rows_copy(i, of):
        at = rows_s.at[i // planes, pl.ds(of * half + i % planes * pairs, pairs)]
        return remote(at, at, rows_ss.at[i], rows_rs.at[i], sibling)

    def collect(j):
        for i in groups[j]:
            for d in range(i * R, (i + 1) * R):
                if d:
                    disp_copy(d, me, source(d)).wait_recv()
            arrived = disp_r[pl.ds(behind_y[i] * R, R)].reshape(tile, piece)
            ordered = jnp.dot(perm_s[0], arrived, preferred_element_type=F32).astype(BF)
            at = pl.ds(pl.multiple_of(pool * half + i % planes * pairs, pairs), pairs)
            for c in range(CHUNKS):
                rows_s[j, at, c * piece : (c + 1) * piece] = ordered[c * pairs : (c + 1) * pairs]
            rows_copy(i, pool).start()

    hidden = act_s.shape[1]
    step = min(256, hidden)

    def half_copy(j, n):
        return remote(
            half_s.at[j, n, 1 - pool], half_r.at[j, n], half_ss.at[j, n], half_rs.at[j, n], sibling
        )

    def apply(j):
        for i in groups[j]:
            rows_copy(i, 1 - pool).wait_recv()
        if j == 0:
            loads[4].wait()
            loads[5].wait()

        def expand(n, carry):
            at = pl.ds(pl.multiple_of(n * step, step), step)
            gate = jnp.dot(rows_s[j], wg_s[0, :, at], preferred_element_type=F32)
            upper = jnp.dot(rows_s[j], wu_s[0, :, at], preferred_element_type=F32)
            act_s[:, at] = (gate / (1.0 + jnp.exp(-gate)) * upper).astype(BF)
            return carry

        lax.fori_loop(0, hidden // step, expand, 0)
        if j == 0:
            loads[6].wait()

        def contract(n, carry):
            at = pl.ds(pl.multiple_of(n * piece, piece), piece)
            out = jnp.dot(act_s[...], wd_s[0, :, at], preferred_element_type=F32)
            half_s[j, n, 0] = out[:half].astype(BF)
            half_s[j, n, 1] = out[half:].astype(BF)
            half_copy(j, n).start()
            return carry

        lax.fori_loop(0, CHUNKS, contract, 0)

    def give_back(j):
        for n in range(CHUNKS):
            half_copy(j, n).wait_recv()
            sum_s[n] = (half_s[j, n, pool].astype(F32) + half_r[j, n].astype(F32)).astype(BF)
        for i in groups[j]:
            k = i % planes * pairs
            stacked = sum_s[:, k : k + pairs, :].reshape(tile, piece)
            out = jnp.dot(perm_s[1], stacked, preferred_element_type=F32).astype(BF)
            back_s[pl.ds(behind_y[i] * R, R)] = out.reshape(R, PAIR, piece)
        for d in sent(j, -1):
            back_copy(d, to(d), me).start()

    collect(0)
    apply(0)
    collect(1)
    give_back(0)
    apply(1)
    give_back(1)
    back_r[me] = back_s[me]
    for d in far:
        back_copy(d, me, source(d)).wait_recv()
    returned = back_r[...].reshape(E * PAIR, piece)
    mixed = jnp.dot(comb_s[0], returned, preferred_element_type=F32) + jnp.dot(
        comb_s[1], returned, preferred_element_type=F32
    )
    for c in range(CHUNKS):
        mix_ref[:, c * piece : (c + 1) * piece] = mixed[c * few : (c + 1) * few].astype(BF)

    for h in range(2):
        for k in range(1, wide):
            for copy in part_copy(h, k) + next_copy(h, k):
                copy.wait_send()
            pass_copy(h, k, here[1 - h]).wait_send()
            wide_copy(h, k, here[h]).wait_send()
    for d in far:
        cols_copy(d, to(d), me).wait_send()
        disp_copy(d, to(d), me).wait_send()
        back_copy(d, to(d), me).wait_send()
    for i in range(G):
        rows_copy(i, pool).wait_send()
    for j in range(2):
        for n in range(CHUNKS):
            half_copy(j, n).wait_send()


def per_device(
    G, R,
    queries, keys, values, hidden_in, o_weight, norm_gain, routes, route_weights,
    w_gate, w_up, w_down,
):
    E = G * R
    rows_all, width = queries.shape
    few, model = hidden_in.shape
    block = o_weight.shape[1]
    hidden = w_gate.shape[2]
    heads = width // HEAD_DIM
    share = rows_all // R
    lanes = share * heads // 2
    wide = math.isqrt(R)
    piece = model // CHUNKS
    side = E * SLOTS

    vmem = pl.BlockSpec(memory_space=pltpu.VMEM)
    smem = pl.BlockSpec(memory_space=pltpu.SMEM)
    anywhere = pl.BlockSpec(memory_space=pl.ANY)
    dma = pltpu.SemaphoreType.DMA
    scratch = [
        pltpu.VMEM(queries.shape, BF),
        pltpu.VMEM(keys.shape, BF),
        pltpu.VMEM(values.shape, BF),
        pltpu.VMEM(o_weight.shape, BF),
        pltpu.VMEM(w_gate.shape, BF),
        pltpu.VMEM(w_up.shape, BF),
        pltpu.VMEM(w_down.shape, BF),
        dma((7,)),
        pltpu.SemaphoreType.REGULAR((2,)),
        pltpu.VMEM((2, wide, wide * lanes, HEAD_DIM), BF),
        pltpu.VMEM((2, wide, 8, wide * lanes), F32),
        pltpu.VMEM((2, wide - 1, wide * lanes, HEAD_DIM), BF),
        pltpu.VMEM((2, wide - 1, 8, wide * lanes), F32),
        pltpu.VMEM((2, wide, lanes, HEAD_DIM), BF),
        pltpu.VMEM((2, wide, 8, lanes), F32),
        pltpu.VMEM((2, wide - 1, lanes, HEAD_DIM), BF),
        pltpu.VMEM((2, wide - 1, 8, lanes), F32),
        pltpu.VMEM((2, wide, wide, share, width // 2), BF),
        pltpu.VMEM((E, few, block), F32),
        pltpu.VMEM((E, few, block), F32),
        pltpu.VMEM((E * PAIR, CHUNKS * few), BF),
        pltpu.VMEM((2, CHUNKS * few, E * PAIR), BF),
        pltpu.VMEM((2, R * PAIR, R * PAIR), BF),
        pltpu.VMEM((E, PAIR, piece), BF),
        pltpu.VMEM((E, PAIR, piece), BF),
        pltpu.VMEM((2, side, model), BF),
        pltpu.VMEM((side, hidden), BF),
        pltpu.VMEM((2, CHUNKS, 2, side // 2, piece), BF),
        pltpu.VMEM((2, CHUNKS, side // 2, piece), BF),
        pltpu.VMEM((CHUNKS, side // 2, piece), BF),
        pltpu.VMEM((E, PAIR, piece), BF),
        pltpu.VMEM((E, PAIR, piece), BF),
    ]
    for count in [(2, wide - 1)] * 6 + [E - 1, E - 1, G, (2, CHUNKS), E - 1]:
        shape = count if isinstance(count, tuple) else (count,)
        scratch += [dma(shape), dma(shape)]
    return pl.pallas_call(
        functools.partial(layer, G, R),
        out_shape=[jax.ShapeDtypeStruct(hidden_in.shape, BF)] * 2,
        in_specs=[anywhere] * 4 + [vmem] * 2 + [smem] * 2 + [anywhere] * 3,
        out_specs=[vmem] * 2,
        scratch_shapes=scratch,
        compiler_params=pltpu.CompilerParams(
            collective_id=0, has_side_effects=True, vmem_limit_bytes=58 << 20
        ),
        name="decode_layer",
    )(
        queries, keys, values, o_weight,
        hidden_in, norm_gain, routes, route_weights,
        w_gate, w_up, w_down,
    )


def solution(mesh):
    rows = P(("pool", "grp", "rep"), None)
    return jax.shard_map(
        functools.partial(per_device, mesh.shape["grp"], mesh.shape["rep"]),
        mesh=mesh,
        in_specs=(
            P("pool", "grp"),
            P("rep", "grp"),
            P("rep", "grp"),
            rows,
            P("grp", "rep"),
            P(),
            rows,
            rows,
            P(("grp", "rep"), None, "pool"),
            P(("grp", "rep"), None, "pool"),
            P(("grp", "rep"), "pool", None),
        ),
        out_specs=(rows, rows),
        check_vma=False,
    )
```

```python
import functools
import math

import jax
import jax.numpy as jnp
from jax import lax
from jax.experimental import pallas as pl
from jax.experimental.pallas import tpu as pltpu
from jax.sharding import PartitionSpec as P

HEAD_DIM = 128
CHUNKS = 8
SLOTS = 2
PAIR = CHUNKS * SLOTS
MESH = pl.DeviceIdType.MESH
BF = jnp.bfloat16
F32 = jnp.float32


def remote(src, dst, send, recv, where):
    return pltpu.make_async_remote_copy(
        src_ref=src,
        dst_ref=dst,
        send_sem=send,
        recv_sem=recv,
        device_id=where,
        device_id_type=MESH,
    )


def layer(
    G, R,
    q_hbm, k_hbm, v_hbm, ow_hbm, hidden_ref, gain_ref, routes_ref, weights_ref, wg_hbm, wu_hbm, wd_hbm,
    out_ref,
    q_s, k_s, v_s, ow_s, wg_s, wu_s, wd_s, load_sem,
    known, part_s, stat_s, part_r, stat_r, next_s, tops_s, next_r, tops_r, attn_s,
    proj_f, proj_s, proj_r, cols_s, cols_r, sel_s, comb_s, perm_s,
    disp_s, disp_r, rows_s, act_s, half_s, half_r, sum_s, back_s, back_r,
    part_ss, part_rs, stat_ss, stat_rs, next_ss, next_rs, tops_ss, tops_rs,
    pass_ss, pass_rs, wide_ss, wide_rs,
    proj_ss, proj_rs, cols_ss, cols_rs, disp_ss, disp_rs,
    rows_ss, rows_rs, half_ss, half_rs, back_ss, back_rs,
):
    pool, grp, rep = lax.axis_index("pool"), lax.axis_index("grp"), lax.axis_index("rep")
    E = G * R
    wide = math.isqrt(R)
    me = grp * R + rep
    sibling = (1 - pool, grp, rep)

    way = 1 - 2 * pool
    x, z = rep // wide, rep % wide
    ahead_y = [lax.rem(grp + way * d + G, G) for d in range(G)]
    behind_y = [lax.rem(grp - way * d + G, G) for d in range(G)]
    ahead_x = [lax.rem(x + way * d + wide, wide) * wide for d in range(wide)]
    behind_x = [lax.rem(x - way * d + wide, wide) * wide for d in range(wide)]
    ahead_z = [lax.rem(z + way * d + wide, wide) for d in range(wide)]
    behind_z = [lax.rem(z - way * d + wide, wide) for d in range(wide)]

    def ahead(d):
        d, plane = d % R, d // R
        return ahead_y[plane], ahead_x[d // wide] + ahead_z[d % wide]

    def behind(d):
        d, plane = d % R, d // R
        return behind_y[plane], behind_x[d // wide] + behind_z[d % wide]

    far = [i * (E // 2 - 5) % E for i in range(1, E)]

    loads = [
        pltpu.make_async_copy(src, dst, load_sem.at[i])
        for i, (src, dst) in enumerate(
            (
                (q_hbm, q_s),
                (k_hbm, k_s),
                (v_hbm, v_s),
                (ow_hbm, ow_s),
                (wg_hbm, wg_s),
                (wu_hbm, wu_s),
                (wd_hbm, wd_s),
            )
        )
    ]
    for load in loads[:3]:
        load.start()

    barrier = pltpu.get_barrier_semaphore()
    along_x = [d * wide for d in range(1, wide)]
    along_z = list(range(1, wide))
    along_y = [d * R for d in range(1, G)]
    axes = along_x + along_z + along_y

    def greet(sem, shifts):
        for d in shifts:
            pl.semaphore_signal(sem, inc=1, device_id=(pool, *ahead(d)), device_id_type=MESH)

    greet(barrier, axes)
    pl.semaphore_signal(barrier, inc=1, device_id=sibling, device_id_type=MESH)

    for load in loads[:3]:
        load.wait()
    loads[3].start()

    rows_all, width = q_s.shape
    heads = width // HEAD_DIM // 2
    share = rows_all // R
    lanes = share * heads
    scale = HEAD_DIM ** (-0.5)
    few, topk = routes_ref.shape
    firsts, seconds = (along_x, along_z), (along_z, along_x)
    across = ([x * wide for x in range(wide)], list(range(wide)))
    orders = [*range(2, wide), 1, 0] if wide > 2 else [1, 0]
    here = (x, z)

    def part_copy(h, k):
        where = (pool, *ahead(firsts[h][k - 1]))
        return [
            remote(a.at[h, k], b.at[h, k - 1], c.at[h, k - 1], d.at[h, k - 1], where)
            for a, b, c, d in ((part_s, part_r, part_ss, part_rs), (stat_s, stat_r, stat_ss, stat_rs))
        ]

    def attend(h, k):
        start = ahead_x[k] if h == 0 else ahead_z[k]
        for pair in range(0, wide, 2):
            pieces = []
            for other in (pair, pair + 1):
                row = pl.multiple_of((start + across[1 - h][other]) * share, share)
                for head in range(h * heads, (h + 1) * heads):
                    pieces.append(
                        q_s[pl.ds(row, share), head * HEAD_DIM : (head + 1) * HEAD_DIM]
                    )
            query = jnp.concatenate(pieces, axis=0)
            scores = lax.dot_general(
                query, k_s[...], (((1,), (1,)), ((), ())), preferred_element_type=F32
            )
            top = jnp.max(scores, axis=1, keepdims=True)
            probs = jnp.exp((scores - top) * scale)
            total = jnp.sum(probs, axis=1, keepdims=True)
            part = jnp.dot(probs.astype(BF), v_s[...], preferred_element_type=F32)
            part_s[h, k, pair * lanes : (pair + 2) * lanes] = part.astype(BF)
            first = lax.broadcasted_iota(jnp.int32, (2 * lanes, 128), 1) < 4
            stat_s[h, k, :, pair * lanes : (pair + 2) * lanes] = (
                jnp.where(first, top, total).T[:8]
            )

    met = False
    for k in orders:
        for h in range(2):
            attend(h, k)
            if not met:
                pl.semaphore_wait(barrier, len(axes) + 1)
                greet(known.at[0], along_x)
                met = True
            if k:
                for copy in part_copy(h, k):
                    copy.start()

    def merged(parts, stats, divide):
        top = functools.reduce(jnp.maximum, [stat[0:1] for stat in stats])
        factors = [jnp.exp((stat[0:1] - top) * scale) for stat in stats]
        total = functools.reduce(
            jnp.add, [stat[4:5] * factor for stat, factor in zip(stats, factors)]
        )
        if divide:
            factors = [factor / total for factor in factors]
        empty = jnp.zeros((128 - len(stats), top.shape[1]), F32)
        columns = jnp.concatenate(factors + [empty], axis=0).T
        out = functools.reduce(
            jnp.add, [part.astype(F32) * columns[:, i : i + 1] for i, part in enumerate(parts)]
        )
        return out.astype(BF), top, total

    def next_copy(h, k):
        d = seconds[h][k - 1]
        there = (ahead_z[k] if h == 0 else ahead_x[k] // wide)
        where = (pool, *ahead(d))
        return [
            remote(a.at[h, there], b.at[h, k - 1], c.at[h, k - 1], d.at[h, k - 1], where)
            for a, b, c, d in ((next_s, next_r, next_ss, next_rs), (tops_s, tops_r, tops_ss, tops_rs))
        ]

    for h in range(2):
        for k in range(1, wide):
            for copy in part_copy(h, k):
                copy.wait_recv()
        out, top, total = merged(
            [part_s[h, 0]] + [part_r[h, k] for k in range(wide - 1)],
            [stat_s[h, 0]] + [stat_r[h, k] for k in range(wide - 1)],
            False,
        )
        first = lax.broadcasted_iota(jnp.int32, (8, lanes), 0) < 4
        for other in range(wide):
            at = slice(other * lanes, (other + 1) * lanes)
            next_s[h, other] = out[at]
            tops_s[h, other] = jnp.where(first, top[:, at], total[:, at])
        for k in range(1, wide):
            for copy in next_copy(h, k):
                copy.start()
    pl.semaphore_wait(known.at[0], wide - 1)
    greet(known.at[1], along_y)

    def pass_copy(h, k, block):
        at = attn_s.at[h, here[h], block]
        where = (pool, *ahead(seconds[h][k - 1]))
        return remote(at, at, pass_ss.at[h, k - 1], pass_rs.at[h, k - 1], where)

    def wide_copy(h, k, block):
        at = attn_s.at[h, block]
        where = (pool, *ahead(firsts[h][k - 1]))
        return remote(at, at, wide_ss.at[h, k - 1], wide_rs.at[h, k - 1], where)

    behind_of = (behind_z, [v // wide for v in behind_x])
    for h in range(2):
        for k in range(1, wide):
            for copy in next_copy(h, k):
                copy.wait_recv()
        mine = here[1 - h]
        out, _, _ = merged(
            [next_s[h, mine]] + [next_r[h, k] for k in range(wide - 1)],
            [tops_s[h, mine]] + [tops_r[h, k] for k in range(wide - 1)],
            True,
        )
        for head in range(heads):
            attn_s[h, here[h], mine, :, head * HEAD_DIM : (head + 1) * HEAD_DIM] = out[
                head * share : (head + 1) * share
            ]
        for k in range(1, wide):
            pass_copy(h, k, mine).start()
    for load in loads[4:]:
        load.start()

    lane = lax.broadcasted_iota(jnp.int32, (1, E * PAIR), 1)
    expert, chunk, slot = lane // PAIR, lane % PAIR // SLOTS, lane % SLOTS
    before = jnp.zeros((1, E * PAIR), jnp.int32)
    taken, weights = [], []
    for r in range(few):
        named, weight = jnp.zeros_like(before), jnp.zeros(before.shape, F32)
        for k in range(topk):
            hit = expert == routes_ref[r, k]
            named = jnp.where(hit, 1, named)
            weight = jnp.where(hit, weights_ref[r, k], weight)
        use = jnp.where(before == slot, named, 0).astype(F32)
        taken.append(use)
        weights.append(use * weight)
        before = before + named
    of_row = lax.broadcasted_iota(jnp.int32, (CHUNKS * few, E * PAIR), 0) // few
    select = jnp.where(of_row == chunk, jnp.concatenate(taken * CHUNKS, axis=0), 0.0)
    sel_s[...] = select.T.astype(BF)
    combine = jnp.where(of_row == chunk, jnp.concatenate(weights * CHUNKS, axis=0), 0.0)
    high = combine.astype(BF)
    comb_s[0] = high
    comb_s[1] = (combine - high.astype(F32)).astype(BF)

    tile = R * PAIR
    pairs = R * SLOTS
    row = lax.broadcasted_iota(jnp.int32, (tile, tile), 0)
    col = lax.broadcasted_iota(jnp.int32, (tile, tile), 1)

    def moved(i):
        return lax.rem(i, pairs) // SLOTS * PAIR + i // pairs * SLOTS + lax.rem(i, SLOTS)

    perm_s[0] = jnp.where(col == moved(row), 1.0, 0.0).astype(BF)
    perm_s[1] = jnp.where(row == moved(col), 1.0, 0.0).astype(BF)

    for h in range(2):
        for k in range(1, wide):
            pass_copy(h, k, behind_of[h][k]).wait_recv()
        for k in range(1, wide):
            wide_copy(h, k, here[h]).start()
    for h in range(2):
        for k in range(1, wide):
            wide_copy(h, k, behind_of[1 - h][k]).wait_recv()
    loads[3].wait()
    middle = width // 2
    straight, turned = [
        jnp.dot(
            attn_s[h].reshape(rows_all, middle),
            ow_s[h * middle : (h + 1) * middle, :],
            preferred_element_type=F32,
        )
        for h in range(2)
    ]
    tall = rows_all // G
    for g in range(G):
        other = jnp.concatenate(
            [
                turned[(b % wide * wide + b // wide) * share :][:share]
                for b in range(g * tall // share, (g + 1) * tall // share)
            ],
            axis=0,
        )
        proj_f[g] = straight[g * tall : (g + 1) * tall] + other
        proj_s[g] = proj_f[g].astype(BF)

    def proj_copy(d):
        there = ahead_y[d]
        return remote(
            proj_s.at[there], proj_r.at[d - 1], proj_ss.at[d - 1], proj_rs.at[d - 1],
            (pool, there, rep),
        )

    for d in range(1, G):
        proj_copy(d).start()
    summed = proj_f[grp]
    for d in range(1, G):
        proj_copy(d).wait_recv()
        summed = summed + proj_r[d - 1].astype(F32)
    summed = summed.astype(BF).astype(F32)
    for j in range(R):
        cols_s[j] = summed[j * few : (j + 1) * few]

    def pair_copy(src, dst, send, recv, d, a, b):
        return remote(
            src.at[a], dst.at[b], send.at[d - 1], recv.at[d - 1], (pool, *ahead(d))
        )

    def disp_copy(d, a, b):
        return pair_copy(disp_s, disp_r, disp_ss, disp_rs, d, a, b)

    def back_copy(d, a, b):
        return pair_copy(back_s, back_r, back_ss, back_rs, d, a, b)

    def to(d):
        there, along = ahead(d)
        return there * R + along

    def source(d):
        there, along = behind(d)
        return there * R + along

    near = [i * (R // 2 - 1) % R for i in range(1, R)]

    def cols_copy(d, a, b):
        return pair_copy(cols_s, cols_r, cols_ss, cols_rs, d, a, b)

    for d in near:
        cols_copy(d, ahead(d)[1], rep).start()
    cols_r[rep] = cols_s[rep]
    for d in near:
        cols_copy(d, rep, behind(d)[1]).wait_recv()
    pl.semaphore_wait(known.at[1], G - 1)
    projected = jnp.concatenate([cols_r[j] for j in range(R)], axis=1)
    mid = (hidden_ref[...].astype(F32) + projected).astype(BF)
    wider = mid.astype(F32)
    out_ref[0] = mid
    inverse = lax.rsqrt(jnp.mean(wider * wider, axis=-1, keepdims=True) + 1e-06)
    normed = wider * inverse * gain_ref[...].astype(F32).reshape(1, -1)
    piece = normed.shape[1] // CHUNKS
    pieces = jnp.concatenate(
        [normed[:, c * piece : (c + 1) * piece] for c in range(CHUNKS)], axis=0
    ).astype(BF)

    planes = G // 2
    groups = [range(j * planes, (j + 1) * planes) for j in range(2)]

    def sent(j, sign):
        return [d for d in far if sign * (d // R) % G in groups[j]]

    for j in range(2):
        for i in groups[j]:
            t = ahead_y[i]
            chosen = jnp.dot(
                sel_s[pl.ds(pl.multiple_of(t * tile, tile), tile), :],
                pieces,
                preferred_element_type=F32,
            )
            disp_s[pl.ds(t * R, R)] = chosen.astype(BF).reshape(R, PAIR, piece)
        for d in sent(j, 1):
            disp_copy(d, to(d), me).start()
    disp_r[me] = disp_s[me]
    half = planes * pairs

    def rows_copy(i, of):
        at = rows_s.at[i // planes, pl.ds(of * half + i % planes * pairs, pairs)]
        return remote(at, at, rows_ss.at[i], rows_rs.at[i], sibling)

    def collect(j):
        for i in groups[j]:
            for d in range(i * R, (i + 1) * R):
                if d:
                    disp_copy(d, me, source(d)).wait_recv()
            arrived = disp_r[pl.ds(behind_y[i] * R, R)].reshape(tile, piece)
            ordered = jnp.dot(perm_s[0], arrived, preferred_element_type=F32).astype(BF)
            at = pl.ds(pl.multiple_of(pool * half + i % planes * pairs, pairs), pairs)
            for c in range(CHUNKS):
                rows_s[j, at, c * piece : (c + 1) * piece] = ordered[c * pairs : (c + 1) * pairs]
            rows_copy(i, pool).start()

    hidden = act_s.shape[1]
    step = min(256, hidden)

    def half_copy(j, n):
        return remote(
            half_s.at[j, n, 1 - pool], half_r.at[j, n], half_ss.at[j, n], half_rs.at[j, n], sibling
        )

    def apply(j):
        for i in groups[j]:
            rows_copy(i, 1 - pool).wait_recv()
        if j == 0:
            loads[4].wait()
            loads[5].wait()

        def expand(n, carry):
            at = pl.ds(pl.multiple_of(n * step, step), step)
            gate = jnp.dot(rows_s[j], wg_s[0, :, at], preferred_element_type=F32)
            upper = jnp.dot(rows_s[j], wu_s[0, :, at], preferred_element_type=F32)
            act_s[:, at] = (gate / (1.0 + jnp.exp(-gate)) * upper).astype(BF)
            return carry

        lax.fori_loop(0, hidden // step, expand, 0)
        if j == 0:
            loads[6].wait()

        def contract(n, carry):
            at = pl.ds(pl.multiple_of(n * piece, piece), piece)
            out = jnp.dot(act_s[...], wd_s[0, :, at], preferred_element_type=F32)
            half_s[j, n, 0] = out[:half].astype(BF)
            half_s[j, n, 1] = out[half:].astype(BF)
            half_copy(j, n).start()
            return carry

        lax.fori_loop(0, CHUNKS, contract, 0)

    def give_back(j):
        for n in range(CHUNKS):
            half_copy(j, n).wait_recv()
            sum_s[n] = (half_s[j, n, pool].astype(F32) + half_r[j, n].astype(F32)).astype(BF)
        for i in groups[j]:
            k = i % planes * pairs
            stacked = sum_s[:, k : k + pairs, :].reshape(tile, piece)
            out = jnp.dot(perm_s[1], stacked, preferred_element_type=F32).astype(BF)
            back_s[pl.ds(behind_y[i] * R, R)] = out.reshape(R, PAIR, piece)
        for d in sent(j, -1):
            back_copy(d, to(d), me).start()

    collect(0)
    apply(0)
    collect(1)
    give_back(0)
    apply(1)
    give_back(1)
    back_r[me] = back_s[me]
    for d in far:
        back_copy(d, me, source(d)).wait_recv()
    returned = back_r[...].reshape(E * PAIR, piece)
    mixed = jnp.dot(comb_s[0], returned, preferred_element_type=F32) + jnp.dot(
        comb_s[1], returned, preferred_element_type=F32
    )
    for c in range(CHUNKS):
        out_ref[1, :, c * piece : (c + 1) * piece] = mixed[c * few : (c + 1) * few].astype(BF)

    for h in range(2):
        for k in range(1, wide):
            for copy in part_copy(h, k) + next_copy(h, k):
                copy.wait_send()
            pass_copy(h, k, here[1 - h]).wait_send()
            wide_copy(h, k, here[h]).wait_send()
    for d in range(1, G):
        proj_copy(d).wait_send()
    for d in near:
        cols_copy(d, ahead(d)[1], rep).wait_send()
    for d in far:
        disp_copy(d, to(d), me).wait_send()
        back_copy(d, to(d), me).wait_send()
    for i in range(G):
        rows_copy(i, pool).wait_send()
    for j in range(2):
        for n in range(CHUNKS):
            half_copy(j, n).wait_send()


def per_device(
    G, R,
    queries, keys, values, hidden_in, o_weight, norm_gain, routes, route_weights,
    w_gate, w_up, w_down,
):
    E = G * R
    rows_all, width = queries.shape
    few, model = hidden_in.shape
    block = o_weight.shape[1]
    hidden = w_gate.shape[2]
    heads = width // HEAD_DIM
    share = rows_all // R
    lanes = share * heads // 2
    wide = math.isqrt(R)
    tall = rows_all // G
    piece = model // CHUNKS
    side = E * SLOTS

    vmem = pl.BlockSpec(memory_space=pltpu.VMEM)
    smem = pl.BlockSpec(memory_space=pltpu.SMEM)
    anywhere = pl.BlockSpec(memory_space=pl.ANY)
    dma = pltpu.SemaphoreType.DMA
    scratch = [
        pltpu.VMEM(queries.shape, BF),
        pltpu.VMEM(keys.shape, BF),
        pltpu.VMEM(values.shape, BF),
        pltpu.VMEM(o_weight.shape, BF),
        pltpu.VMEM(w_gate.shape, BF),
        pltpu.VMEM(w_up.shape, BF),
        pltpu.VMEM(w_down.shape, BF),
        dma((7,)),
        pltpu.SemaphoreType.REGULAR((2,)),
        pltpu.VMEM((2, wide, wide * lanes, HEAD_DIM), BF),
        pltpu.VMEM((2, wide, 8, wide * lanes), F32),
        pltpu.VMEM((2, wide - 1, wide * lanes, HEAD_DIM), BF),
        pltpu.VMEM((2, wide - 1, 8, wide * lanes), F32),
        pltpu.VMEM((2, wide, lanes, HEAD_DIM), BF),
        pltpu.VMEM((2, wide, 8, lanes), F32),
        pltpu.VMEM((2, wide - 1, lanes, HEAD_DIM), BF),
        pltpu.VMEM((2, wide - 1, 8, lanes), F32),
        pltpu.VMEM((2, wide, wide, share, width // 2), BF),
        pltpu.VMEM((G, tall, block), F32),
        pltpu.VMEM((G, tall, block), BF),
        pltpu.VMEM((G - 1, tall, block), BF),
        pltpu.VMEM((R, few, block), F32),
        pltpu.VMEM((R, few, block), F32),
        pltpu.VMEM((E * PAIR, CHUNKS * few), BF),
        pltpu.VMEM((2, CHUNKS * few, E * PAIR), BF),
        pltpu.VMEM((2, R * PAIR, R * PAIR), BF),
        pltpu.VMEM((E, PAIR, piece), BF),
        pltpu.VMEM((E, PAIR, piece), BF),
        pltpu.VMEM((2, side, model), BF),
        pltpu.VMEM((side, hidden), BF),
        pltpu.VMEM((2, CHUNKS, 2, side // 2, piece), BF),
        pltpu.VMEM((2, CHUNKS, side // 2, piece), BF),
        pltpu.VMEM((CHUNKS, side // 2, piece), BF),
        pltpu.VMEM((E, PAIR, piece), BF),
        pltpu.VMEM((E, PAIR, piece), BF),
    ]
    for count in [(2, wide - 1)] * 6 + [G - 1, R - 1, E - 1, G, (2, CHUNKS), E - 1]:
        shape = count if isinstance(count, tuple) else (count,)
        scratch += [dma(shape), dma(shape)]
    out = pl.pallas_call(
        functools.partial(layer, G, R),
        out_shape=jax.ShapeDtypeStruct((2, few, model), BF),
        in_specs=[anywhere] * 4 + [vmem] * 2 + [smem] * 2 + [anywhere] * 3,
        out_specs=vmem,
        scratch_shapes=scratch,
        compiler_params=pltpu.CompilerParams(
            collective_id=0, has_side_effects=True, vmem_limit_bytes=58 << 20
        ),
        name="decode_layer",
    )(
        queries, keys, values, o_weight,
        hidden_in, norm_gain, routes, route_weights,
        w_gate, w_up, w_down,
    )
    return out[0], out[1]


def solution(mesh):
    rows = P(("pool", "grp", "rep"), None)
    return jax.shard_map(
        functools.partial(per_device, mesh.shape["grp"], mesh.shape["rep"]),
        mesh=mesh,
        in_specs=(
            P("pool", "grp"),
            P("rep", "grp"),
            P("rep", "grp"),
            rows,
            P("grp", "rep"),
            P(),
            rows,
            rows,
            P(("grp", "rep"), None, "pool"),
            P(("grp", "rep"), None, "pool"),
            P(("grp", "rep"), "pool", None),
        ),
        out_specs=(rows, rows),
        check_vma=False,
    )
```

```python
import functools
import math

import jax
import jax.numpy as jnp
from jax import lax
from jax.experimental import pallas as pl
from jax.experimental.pallas import tpu as pltpu
from jax.sharding import PartitionSpec as P

HEAD_DIM = 128
LOG2E = 1.4426950408889634
CHUNKS = 8
SLOTS = 2
PAIR = CHUNKS * SLOTS
MESH = pl.DeviceIdType.MESH
BF = jnp.bfloat16
F32 = jnp.float32


def remote(src, dst, send, recv, where):
    return pltpu.make_async_remote_copy(
        src_ref=src,
        dst_ref=dst,
        send_sem=send,
        recv_sem=recv,
        device_id=where,
        device_id_type=MESH,
    )


def layer(
    G, R,
    q_hbm, k_hbm, v_hbm, ow_hbm, hidden_ref, gain_ref, routes_ref, weights_ref, wg_hbm, wu_hbm, wd_hbm,
    out_ref,
    q_s, k_s, v_s, value_s, ow_s, wg_s, wu_s, wd_s, load_sem,
    known, part_s, stat_s, part_r, stat_r, next_s, tops_s, next_r, tops_r, attn_s,
    proj_f, proj_s, proj_r, cols_s, cols_r, sel_s, comb_s, perm_s,
    disp_s, disp_r, rows_s, act_s, half_s, half_r, sum_s, back_s, back_r,
    part_ss, part_rs, stat_ss, stat_rs, next_ss, next_rs, tops_ss, tops_rs,
    pass_ss, pass_rs, wide_ss, wide_rs,
    proj_ss, proj_rs, cols_ss, cols_rs, disp_ss, disp_rs,
    rows_ss, rows_rs, half_ss, half_rs, back_ss, back_rs,
):
    pool, grp, rep = lax.axis_index("pool"), lax.axis_index("grp"), lax.axis_index("rep")
    E = G * R
    wide = math.isqrt(R)
    me = grp * R + rep
    sibling = (1 - pool, grp, rep)

    way = 1 - 2 * pool
    x, z = rep // wide, rep % wide
    ahead_y = [lax.rem(grp + way * d + G, G) for d in range(G)]
    behind_y = [lax.rem(grp - way * d + G, G) for d in range(G)]
    ahead_x = [lax.rem(x + way * d + wide, wide) * wide for d in range(wide)]
    behind_x = [lax.rem(x - way * d + wide, wide) * wide for d in range(wide)]
    ahead_z = [lax.rem(z + way * d + wide, wide) for d in range(wide)]
    behind_z = [lax.rem(z - way * d + wide, wide) for d in range(wide)]

    def ahead(d):
        d, plane = d % R, d // R
        return ahead_y[plane], ahead_x[d // wide] + ahead_z[d % wide]

    def behind(d):
        d, plane = d % R, d // R
        return behind_y[plane], behind_x[d // wide] + behind_z[d % wide]

    far = [i * (E // 2 - 5) % E for i in range(1, E)]

    loads = [
        pltpu.make_async_copy(src, dst, load_sem.at[i])
        for i, (src, dst) in enumerate(
            (
                (q_hbm, q_s),
                (k_hbm, k_s),
                (v_hbm, v_s),
                (ow_hbm, ow_s),
                (wg_hbm, wg_s),
                (wu_hbm, wu_s),
                (wd_hbm, wd_s),
            )
        )
    ]
    for load in loads[:3]:
        load.start()

    barrier = pltpu.get_barrier_semaphore()
    along_x = [d * wide for d in range(1, wide)]
    along_z = list(range(1, wide))
    along_y = [d * R for d in range(1, G)]
    axes = along_x + along_z + along_y

    def greet(sem, shifts):
        for d in shifts:
            pl.semaphore_signal(sem, inc=1, device_id=(pool, *ahead(d)), device_id_type=MESH)

    greet(barrier, axes)
    pl.semaphore_signal(barrier, inc=1, device_id=sibling, device_id_type=MESH)

    for load in loads[:3]:
        load.wait()
    loads[3].start()
    value_s[:, :HEAD_DIM] = v_s[...]
    value_s[:, HEAD_DIM:] = jnp.ones_like(v_s)

    rows_all, width = q_s.shape
    heads = width // HEAD_DIM // 2
    share = rows_all // R
    lanes = share * heads
    scale = HEAD_DIM ** (-0.5)
    few, topk = routes_ref.shape
    firsts, seconds = (along_x, along_z), (along_z, along_x)
    across = ([x * wide for x in range(wide)], list(range(wide)))
    orders = [*range(2, wide), 1, 0] if wide > 2 else [1, 0]
    here = (x, z)

    def part_copy(h, k):
        where = (pool, *ahead(firsts[h][k - 1]))
        return [
            remote(a.at[h, k], b.at[h, k - 1], c.at[h, k - 1], d.at[h, k - 1], where)
            for a, b, c, d in ((part_s, part_r, part_ss, part_rs), (stat_s, stat_r, stat_ss, stat_rs))
        ]

    def attend(h, k):
        start = ahead_x[k] if h == 0 else ahead_z[k]
        for pair in range(0, wide, 2):
            pieces = []
            for other in (pair, pair + 1):
                row = pl.multiple_of((start + across[1 - h][other]) * share, share)
                for head in range(h * heads, (h + 1) * heads):
                    pieces.append(
                        q_s[pl.ds(row, share), head * HEAD_DIM : (head + 1) * HEAD_DIM]
                    )
            query = jnp.concatenate(pieces, axis=0)
            scores = lax.dot_general(
                query, k_s[...], (((1,), (1,)), ((), ())), preferred_element_type=F32
            )
            top = jnp.max(scores, axis=1, keepdims=True)
            probs = jnp.exp2((scores - top) * (scale * LOG2E)).astype(BF)
            part = jnp.dot(probs, value_s[...], preferred_element_type=F32)
            total = part[:, HEAD_DIM:]
            part_s[h, k, pair * lanes : (pair + 2) * lanes] = part[:, :HEAD_DIM].astype(BF)
            first = lax.broadcasted_iota(jnp.int32, (2 * lanes, 128), 1) < 4
            stat_s[h, k, :, pair * lanes : (pair + 2) * lanes] = (
                jnp.where(first, top, total).T[:8]
            )

    met = False
    for k in orders:
        for h in range(2):
            attend(h, k)
        if not met:
            pl.semaphore_wait(barrier, len(axes) + 1)
            greet(known.at[0], along_x)
            met = True
        if k:
            for h in range(2):
                for copy in part_copy(h, k):
                    copy.start()

    def merged(parts, stats, divide):
        top = functools.reduce(jnp.maximum, [stat[0:1] for stat in stats])
        factors = [jnp.exp((stat[0:1] - top) * scale) for stat in stats]
        total = functools.reduce(
            jnp.add, [stat[4:5] * factor for stat, factor in zip(stats, factors)]
        )
        if divide:
            factors = [factor / total for factor in factors]
        empty = jnp.zeros((128 - len(stats), top.shape[1]), F32)
        columns = jnp.concatenate(factors + [empty], axis=0).T
        out = functools.reduce(
            jnp.add, [part.astype(F32) * columns[:, i : i + 1] for i, part in enumerate(parts)]
        )
        return out.astype(BF), top, total

    def next_copy(h, k):
        d = seconds[h][k - 1]
        there = (ahead_z[k] if h == 0 else ahead_x[k] // wide)
        where = (pool, *ahead(d))
        return [
            remote(a.at[h, there], b.at[h, k - 1], c.at[h, k - 1], d.at[h, k - 1], where)
            for a, b, c, d in ((next_s, next_r, next_ss, next_rs), (tops_s, tops_r, tops_ss, tops_rs))
        ]

    for h in range(2):
        for k in range(1, wide):
            for copy in part_copy(h, k):
                copy.wait_recv()
        out, top, total = merged(
            [part_s[h, 0]] + [part_r[h, k] for k in range(wide - 1)],
            [stat_s[h, 0]] + [stat_r[h, k] for k in range(wide - 1)],
            False,
        )
        first = lax.broadcasted_iota(jnp.int32, (8, lanes), 0) < 4
        for other in range(wide):
            at = slice(other * lanes, (other + 1) * lanes)
            next_s[h, other] = out[at]
            tops_s[h, other] = jnp.where(first, top[:, at], total[:, at])
        for k in range(1, wide):
            for copy in next_copy(h, k):
                copy.start()
    pl.semaphore_wait(known.at[0], wide - 1)
    greet(known.at[1], along_y)

    def pass_copy(h, k, block):
        at = attn_s.at[h, here[h], block]
        where = (pool, *ahead(seconds[h][k - 1]))
        return remote(at, at, pass_ss.at[h, k - 1], pass_rs.at[h, k - 1], where)

    def wide_copy(h, k, block):
        at = attn_s.at[h, block]
        where = (pool, *ahead(firsts[h][k - 1]))
        return remote(at, at, wide_ss.at[h, k - 1], wide_rs.at[h, k - 1], where)

    behind_of = (behind_z, [v // wide for v in behind_x])
    for h in range(2):
        for k in range(1, wide):
            for copy in next_copy(h, k):
                copy.wait_recv()
        mine = here[1 - h]
        out, _, _ = merged(
            [next_s[h, mine]] + [next_r[h, k] for k in range(wide - 1)],
            [tops_s[h, mine]] + [tops_r[h, k] for k in range(wide - 1)],
            True,
        )
        for head in range(heads):
            attn_s[h, here[h], mine, :, head * HEAD_DIM : (head + 1) * HEAD_DIM] = out[
                head * share : (head + 1) * share
            ]
        for k in range(1, wide):
            pass_copy(h, k, mine).start()
    for load in loads[4:]:
        load.start()

    lane = lax.broadcasted_iota(jnp.int32, (1, E * PAIR), 1)
    expert, chunk, slot = lane // PAIR, lane % PAIR // SLOTS, lane % SLOTS
    before = jnp.zeros((1, E * PAIR), jnp.int32)
    taken, weights = [], []
    for r in range(few):
        named, weight = jnp.zeros_like(before), jnp.zeros(before.shape, F32)
        for k in range(topk):
            hit = expert == routes_ref[r, k]
            named = jnp.where(hit, 1, named)
            weight = jnp.where(hit, weights_ref[r, k], weight)
        use = jnp.where(before == slot, named, 0).astype(F32)
        taken.append(use)
        weights.append(use * weight)
        before = before + named
    of_row = lax.broadcasted_iota(jnp.int32, (CHUNKS * few, E * PAIR), 0) // few
    select = jnp.where(of_row == chunk, jnp.concatenate(taken * CHUNKS, axis=0), 0.0)
    sel_s[...] = select.T.astype(BF)
    combine = jnp.where(of_row == chunk, jnp.concatenate(weights * CHUNKS, axis=0), 0.0)
    high = combine.astype(BF)
    comb_s[0] = high
    comb_s[1] = (combine - high.astype(F32)).astype(BF)

    tile = R * PAIR
    pairs = R * SLOTS
    row = lax.broadcasted_iota(jnp.int32, (tile, tile), 0)
    col = lax.broadcasted_iota(jnp.int32, (tile, tile), 1)

    def moved(i):
        return lax.rem(i, pairs) // SLOTS * PAIR + i // pairs * SLOTS + lax.rem(i, SLOTS)

    perm_s[0] = jnp.where(col == moved(row), 1.0, 0.0).astype(BF)
    perm_s[1] = jnp.where(row == moved(col), 1.0, 0.0).astype(BF)

    for h in range(2):
        for k in range(1, wide):
            pass_copy(h, k, behind_of[h][k]).wait_recv()
        for k in range(1, wide):
            wide_copy(h, k, here[h]).start()
    for h in range(2):
        for k in range(1, wide):
            wide_copy(h, k, behind_of[1 - h][k]).wait_recv()
    loads[3].wait()
    middle = width // 2
    straight, turned = [
        jnp.dot(
            attn_s[h].reshape(rows_all, middle),
            ow_s[h * middle : (h + 1) * middle, :],
            preferred_element_type=F32,
        )
        for h in range(2)
    ]
    tall = rows_all // G
    for g in range(G):
        other = jnp.concatenate(
            [
                turned[(b % wide * wide + b // wide) * share :][:share]
                for b in range(g * tall // share, (g + 1) * tall // share)
            ],
            axis=0,
        )
        proj_f[g] = straight[g * tall : (g + 1) * tall] + other
        proj_s[g] = proj_f[g].astype(BF)

    def proj_copy(d):
        there = ahead_y[d]
        return remote(
            proj_s.at[there], proj_r.at[d - 1], proj_ss.at[d - 1], proj_rs.at[d - 1],
            (pool, there, rep),
        )

    for d in range(1, G):
        proj_copy(d).start()
    summed = proj_f[grp]
    for d in range(1, G):
        proj_copy(d).wait_recv()
        summed = summed + proj_r[d - 1].astype(F32)
    summed = summed.astype(BF).astype(F32)
    for j in range(R):
        cols_s[j] = summed[j * few : (j + 1) * few]

    def pair_copy(src, dst, send, recv, d, a, b):
        return remote(
            src.at[a], dst.at[b], send.at[d - 1], recv.at[d - 1], (pool, *ahead(d))
        )

    def disp_copy(d, a, b):
        return pair_copy(disp_s, disp_r, disp_ss, disp_rs, d, a, b)

    def back_copy(d, a, b):
        return pair_copy(back_s, back_r, back_ss, back_rs, d, a, b)

    def to(d):
        there, along = ahead(d)
        return there * R + along

    def source(d):
        there, along = behind(d)
        return there * R + along

    near = [i * (R // 2 - 1) % R for i in range(1, R)]

    def cols_copy(d, a, b):
        return pair_copy(cols_s, cols_r, cols_ss, cols_rs, d, a, b)

    for d in near:
        cols_copy(d, ahead(d)[1], rep).start()
    cols_r[rep] = cols_s[rep]
    for d in near:
        cols_copy(d, rep, behind(d)[1]).wait_recv()
    pl.semaphore_wait(known.at[1], G - 1)
    projected = jnp.concatenate([cols_r[j] for j in range(R)], axis=1)
    mid = (hidden_ref[...].astype(F32) + projected).astype(BF)
    wider = mid.astype(F32)
    out_ref[0] = mid
    inverse = lax.rsqrt(jnp.mean(wider * wider, axis=-1, keepdims=True) + 1e-06)
    normed = wider * inverse * gain_ref[...].astype(F32).reshape(1, -1)
    piece = normed.shape[1] // CHUNKS
    pieces = jnp.concatenate(
        [normed[:, c * piece : (c + 1) * piece] for c in range(CHUNKS)], axis=0
    ).astype(BF)

    groups = [[i for i in range(G) if i != G // 2], [G // 2]]
    half = [len(group) * pairs for group in groups]
    base = [0, 2 * half[0]]

    def sent(j, sign):
        return [d for d in far if sign * (d // R) % G in groups[j]]

    for j in range(2):
        for i in groups[j]:
            t = ahead_y[i]
            chosen = jnp.dot(
                sel_s[pl.ds(pl.multiple_of(t * tile, tile), tile), :],
                pieces,
                preferred_element_type=F32,
            )
            disp_s[pl.ds(t * R, R)] = chosen.astype(BF).reshape(R, PAIR, piece)
        for d in sent(j, 1):
            disp_copy(d, to(d), me).start()
    disp_r[me] = disp_s[me]
    def rows_at(i, of):
        j = int(i not in groups[0])
        first = base[j] + of * half[j] + groups[j].index(i) * pairs
        return pl.ds(pl.multiple_of(first, pairs), pairs)

    def rows_copy(i, of):
        at = rows_s.at[rows_at(i, of)]
        return remote(at, at, rows_ss.at[i], rows_rs.at[i], sibling)

    def collect(j):
        for i in groups[j]:
            for d in range(i * R, (i + 1) * R):
                if d:
                    disp_copy(d, me, source(d)).wait_recv()
            arrived = disp_r[pl.ds(behind_y[i] * R, R)].reshape(tile, piece)
            ordered = jnp.dot(perm_s[0], arrived, preferred_element_type=F32).astype(BF)
            at = rows_at(i, pool)
            for c in range(CHUNKS):
                rows_s[at, c * piece : (c + 1) * piece] = ordered[c * pairs : (c + 1) * pairs]
            rows_copy(i, pool).start()

    hidden = act_s.shape[1]
    step = min(256, hidden)

    def half_copy(j, n):
        at = pl.ds(0, half[j])
        return remote(
            half_s.at[j, n, 1 - pool, at], half_r.at[j, n, at],
            half_ss.at[j, n], half_rs.at[j, n], sibling,
        )

    def apply(j):
        for i in groups[j]:
            rows_copy(i, 1 - pool).wait_recv()
        mine = slice(base[j], base[j] + 2 * half[j])
        both = slice(0, 2 * half[j])
        if j == 0:
            loads[4].wait()
            loads[5].wait()

        def expand(n, carry):
            at = pl.ds(pl.multiple_of(n * step, step), step)
            gate = jnp.dot(rows_s[mine], wg_s[0, :, at], preferred_element_type=F32)
            upper = jnp.dot(rows_s[mine], wu_s[0, :, at], preferred_element_type=F32)
            act_s[both, at] = (gate / (1.0 + jnp.exp(-gate)) * upper).astype(BF)
            return carry

        lax.fori_loop(0, hidden // step, expand, 0, unroll=True)
        if j == 0:
            loads[6].wait()

        def contract(n, carry):
            at = pl.ds(pl.multiple_of(n * piece, piece), piece)
            out = jnp.dot(act_s[both], wd_s[0, :, at], preferred_element_type=F32)
            half_s[j, n, 0, : half[j]] = out[: half[j]].astype(BF)
            half_s[j, n, 1, : half[j]] = out[half[j] :].astype(BF)
            half_copy(j, n).start()
            return carry

        lax.fori_loop(0, CHUNKS, contract, 0, unroll=4)

    def give_back(j):
        for n in range(CHUNKS):
            half_copy(j, n).wait_recv()
            sum_s[n, : half[j]] = (
                half_s[j, n, pool, : half[j]].astype(F32) + half_r[j, n, : half[j]].astype(F32)
            ).astype(BF)
        for i in groups[j]:
            k = groups[j].index(i) * pairs
            stacked = sum_s[:, k : k + pairs, :].reshape(tile, piece)
            out = jnp.dot(perm_s[1], stacked, preferred_element_type=F32).astype(BF)
            back_s[pl.ds(behind_y[i] * R, R)] = out.reshape(R, PAIR, piece)
        for d in sent(j, -1):
            back_copy(d, to(d), me).start()

    for h in range(2):
        for k in range(1, wide):
            for copy in part_copy(h, k) + next_copy(h, k):
                copy.wait_send()
            pass_copy(h, k, here[1 - h]).wait_send()
            wide_copy(h, k, here[h]).wait_send()
    for d in range(1, G):
        proj_copy(d).wait_send()
    for d in near:
        cols_copy(d, ahead(d)[1], rep).wait_send()
    collect(0)
    apply(0)
    collect(1)
    give_back(0)
    apply(1)
    give_back(1)
    back_r[me] = back_s[me]
    for d in far:
        disp_copy(d, to(d), me).wait_send()
        back_copy(d, to(d), me).wait_send()
    for i in range(G):
        rows_copy(i, pool).wait_send()
    for j in range(2):
        for n in range(CHUNKS):
            half_copy(j, n).wait_send()
    for d in far:
        back_copy(d, me, source(d)).wait_recv()
    returned = back_r[...].reshape(E * PAIR, piece)
    mixed = jnp.dot(comb_s[0], returned, preferred_element_type=F32) + jnp.dot(
        comb_s[1], returned, preferred_element_type=F32
    )
    for c in range(CHUNKS):
        out_ref[1, :, c * piece : (c + 1) * piece] = mixed[c * few : (c + 1) * few].astype(BF)


def per_device(
    G, R,
    queries, keys, values, hidden_in, o_weight, norm_gain, routes, route_weights,
    w_gate, w_up, w_down,
):
    E = G * R
    rows_all, width = queries.shape
    few, model = hidden_in.shape
    block = o_weight.shape[1]
    hidden = w_gate.shape[2]
    heads = width // HEAD_DIM
    share = rows_all // R
    lanes = share * heads // 2
    wide = math.isqrt(R)
    tall = rows_all // G
    piece = model // CHUNKS
    side = E * SLOTS

    vmem = pl.BlockSpec(memory_space=pltpu.VMEM)
    smem = pl.BlockSpec(memory_space=pltpu.SMEM)
    anywhere = pl.BlockSpec(memory_space=pl.ANY)
    dma = pltpu.SemaphoreType.DMA
    scratch = [
        pltpu.VMEM(queries.shape, BF),
        pltpu.VMEM(keys.shape, BF),
        pltpu.VMEM(values.shape, BF),
        pltpu.VMEM((values.shape[0], 2 * HEAD_DIM), BF),
        pltpu.VMEM(o_weight.shape, BF),
        pltpu.VMEM(w_gate.shape, BF),
        pltpu.VMEM(w_up.shape, BF),
        pltpu.VMEM(w_down.shape, BF),
        dma((7,)),
        pltpu.SemaphoreType.REGULAR((2,)),
        pltpu.VMEM((2, wide, wide * lanes, HEAD_DIM), BF),
        pltpu.VMEM((2, wide, 8, wide * lanes), F32),
        pltpu.VMEM((2, wide - 1, wide * lanes, HEAD_DIM), BF),
        pltpu.VMEM((2, wide - 1, 8, wide * lanes), F32),
        pltpu.VMEM((2, wide, lanes, HEAD_DIM), BF),
        pltpu.VMEM((2, wide, 8, lanes), F32),
        pltpu.VMEM((2, wide - 1, lanes, HEAD_DIM), BF),
        pltpu.VMEM((2, wide - 1, 8, lanes), F32),
        pltpu.VMEM((2, wide, wide, share, width // 2), BF),
        pltpu.VMEM((G, tall, block), F32),
        pltpu.VMEM((G, tall, block), BF),
        pltpu.VMEM((G - 1, tall, block), BF),
        pltpu.VMEM((R, few, block), F32),
        pltpu.VMEM((R, few, block), F32),
        pltpu.VMEM((E * PAIR, CHUNKS * few), BF),
        pltpu.VMEM((2, CHUNKS * few, E * PAIR), BF),
        pltpu.VMEM((2, R * PAIR, R * PAIR), BF),
        pltpu.VMEM((E, PAIR, piece), BF),
        pltpu.VMEM((E, PAIR, piece), BF),
        pltpu.VMEM((2 * side, model), BF),
        pltpu.VMEM((2 * side, hidden), BF),
        pltpu.VMEM((2, CHUNKS, 2, side, piece), BF),
        pltpu.VMEM((2, CHUNKS, side, piece), BF),
        pltpu.VMEM((CHUNKS, side, piece), BF),
        pltpu.VMEM((E, PAIR, piece), BF),
        pltpu.VMEM((E, PAIR, piece), BF),
    ]
    for count in [(2, wide - 1)] * 6 + [G - 1, R - 1, E - 1, G, (2, CHUNKS), E - 1]:
        shape = count if isinstance(count, tuple) else (count,)
        scratch += [dma(shape), dma(shape)]
    out = pl.pallas_call(
        functools.partial(layer, G, R),
        out_shape=jax.ShapeDtypeStruct((2, few, model), BF),
        in_specs=[anywhere] * 4 + [vmem] * 2 + [smem] * 2 + [anywhere] * 3,
        out_specs=vmem,
        scratch_shapes=scratch,
        compiler_params=pltpu.CompilerParams(
            collective_id=0, has_side_effects=True, vmem_limit_bytes=58 << 20
        ),
        name="decode_layer",
    )(
        queries, keys, values, o_weight,
        hidden_in, norm_gain, routes, route_weights,
        w_gate, w_up, w_down,
    )
    return out[0], out[1]


def solution(mesh):
    rows = P(("pool", "grp", "rep"), None)
    return jax.shard_map(
        functools.partial(per_device, mesh.shape["grp"], mesh.shape["rep"]),
        mesh=mesh,
        in_specs=(
            P("pool", "grp"),
            P("rep", "grp"),
            P("rep", "grp"),
            rows,
            P("grp", "rep"),
            P(),
            rows,
            rows,
            P(("grp", "rep"), None, "pool"),
            P(("grp", "rep"), None, "pool"),
            P(("grp", "rep"), "pool", None),
        ),
        out_specs=(rows, rows),
        check_vma=False,
    )
```
